256 devices in a mesh: rec: 32 (over z, y), src: 8 (over x, core).
Axes of the slice: x: 4, y: 4, z: 8, core: 2. Of those that a mesh axis runs over, the one named last changes fastest.
Arguments:
- kernel: float32 [2, 2, 5120, 5120], P(None, None, 'rec', 'src'), may hold values from -0.0625 to 0.0625
- traces: float32 [8, 896, 2, 2, 256], P('src', 'rec')
- acq_lists: int32 [8, 896], P('src', 'rec'), may hold values from 0 to 639, as said below
- counts: int32 [8, 32], P('src', 'rec'), may hold values from 1 to 28, as said below
Outputs:
- solution: float32 [5120, 2, 2, 256], P(('src', 'rec'))
- next_left: float32 [5120, 2, 2, 256], P(('rec', 'src'))
The draws below stay inside these ranges and needn't reach their ends.
Inputs may be any that keep to these rules, and one draw needn't show every extreme that they name: `acq_lists`: an id a * 20 + k names row k of area a. Within each list the first counts[s, r] slots of the blocks name every id exactly once; other slots hold ids to be ignored. No block names more than 1 ids of one area, and every block that names an area names exactly 1 of its ids. `counts`: used slots of a block; in every list some block uses all 28.
All inputs are finite; a program needn't handle non-finite values.
Results may differ from the reference program's by a relative error of at most 0.00026.
Values sent between devices are 32-bit elements; how exact they have to be, the bound alone decides.
A program may use at most 64 MiB of HBM per device.

```python
import math
import jax
import jax.numpy as jnp
from jax import lax

NR = 5120
FREQS = 2
SOURCES = 256
ITERS = 2
AREAS = 32
LISTS = 8
ROWS = 20
PEER = 1
GROUPS = 20
HEAVY = 7
CAP = 28


def one_list(list_key):
    keys = jax.random.split(list_key, 6)
    heavy_count = AREAS // 4
    light_count = AREAS - heavy_count
    total_rows = AREAS * ROWS
    shuffled = jax.random.permutation(keys[0], AREAS)
    heavy = shuffled[:heavy_count]
    light = shuffled[heavy_count:]
    heavy_shift = jax.random.permutation(keys[1], heavy_count)[:HEAVY]
    light_shift = jax.random.permutation(keys[3], light_count)[:GROUPS - HEAVY]
    area_index = jnp.arange(AREAS, dtype=jnp.int32)
    senders = jnp.concatenate([heavy[(area_index[:, None] + heavy_shift[None, :]) % heavy_count], light[(area_index[:, None] + light_shift[None, :]) % light_count]], axis=1)
    row_keys = jax.random.split(keys[4], AREAS)
    group_of_row = jax.vmap(lambda row_key: jax.random.permutation(row_key, ROWS))(row_keys) // PEER
    sender_of = jnp.take_along_axis(senders, group_of_row, axis=1).reshape(-1).astype(jnp.int32)
    identity = jnp.arange(total_rows, dtype=jnp.int32)
    tiebreak = jax.random.permutation(keys[5], total_rows).astype(jnp.int32)
    arranged = jnp.argsort(sender_of * total_rows + tiebreak, stable=True)
    sorted_sender = sender_of[arranged]
    sorted_id = identity[arranged]
    block_counts = jnp.sum((sender_of[None, :] == area_index[:, None]).astype(jnp.int32), axis=1)
    starts = jnp.cumsum(block_counts) - block_counts
    slot_place = identity - starts[sorted_sender]
    filler = jax.random.randint(jax.random.fold_in(list_key, 9), (AREAS, CAP), 0, total_rows)
    table = filler.at[sorted_sender, slot_place].set(sorted_id)
    return (table.reshape(-1).astype(jnp.int32), block_counts.astype(jnp.int32))


def acquisition(base_key):
    list_keys = jax.random.split(base_key, LISTS)
    return jax.vmap(one_list)(list_keys)


def draw_acq_lists(key, part):
    return acquisition(jax.random.fold_in(key, 11))[0]


def draw_counts(key, part):
    return acquisition(jax.random.fold_in(key, 11))[1]


def draw_traces(key, part):
    list_ids = acquisition(jax.random.fold_in(key, 11))[0]
    keys = jax.random.split(jax.random.fold_in(key, 23), 3)
    row_scale = jnp.exp(jax.random.uniform(keys[0], (LISTS, AREAS * ROWS), jnp.float32, 0.0, math.log(10.0)))
    slot_scale = jnp.take_along_axis(row_scale, list_ids, axis=1)
    rising = 1.0 + 2.0 * (list_ids // ROWS).astype(jnp.float32) / (AREAS - 1)
    source_scale = jnp.exp(jax.random.uniform(keys[1], (SOURCES,), jnp.float32, 0.0, math.log(10.0)))
    shape = (LISTS, AREAS * CAP, 2, FREQS, SOURCES)
    base = jax.random.normal(keys[2], shape, jnp.float32)
    values = 0.1 * base * (slot_scale * rising)[:, :, None, None, None] * source_scale[None, None, None, None, :]
    return values.astype(jnp.float32)


def steps_of(own_key, dims, cuts, low, high):
    gain, own = 1.0, jax.random.fold_in(own_key, 6)
    for dim, shards_of in cuts:
        heights = jnp.exp(jax.random.uniform(jax.random.fold_in(own, dim), (shards_of,), jnp.float32, low / len(cuts), high / len(cuts)))
        gain = gain * jnp.repeat(heights, dims[dim] // shards_of).reshape([-1 if axis == dim else 1 for axis in range(len(dims))])
    return gain


def normal_values(rng, extent, spread, reach, cuts=(), kind=jnp.bfloat16):
    factor_of = steps_of(rng, extent, cuts, -0.22, 0.18) if cuts else 1.0
    entries = jax.random.normal(rng, extent, jnp.float32) * spread * factor_of
    return jnp.minimum(jnp.maximum(entries, -reach), reach).astype(kind)


def setup_inputs(seed: int = 0) -> dict:
    streams_of = jax.random.split(jax.random.key(seed), 5)
    return {
        "kernel": normal_values(streams_of[0], (2, FREQS, NR, NR), (2 * NR) ** -0.5, 0.0625, ((2, 32), (3, 8)), jnp.float32),
        "traces": draw_traces(jax.random.fold_in(streams_of[4], 71), 0),
        "acq_lists": draw_acq_lists(jax.random.fold_in(streams_of[4], 71), 0),
        "counts": draw_counts(jax.random.fold_in(streams_of[4], 71), 0),
    }


def kernel_apply(kernel, vector):
    highest = lax.Precision.HIGHEST
    real_part = jnp.einsum('fmc,cfn->mfn', kernel[0], vector[:, 0], precision=highest) - jnp.einsum('fmc,cfn->mfn', kernel[1], vector[:, 1], precision=highest)
    imag_part = jnp.einsum('fmc,cfn->mfn', kernel[0], vector[:, 1], precision=highest) + jnp.einsum('fmc,cfn->mfn', kernel[1], vector[:, 0], precision=highest)
    return jnp.stack([real_part, imag_part], axis=1)

def kernel_adjoint(kernel, vector):
    highest = lax.Precision.HIGHEST
    real_part = jnp.einsum('fmc,mfn->cfn', kernel[0], vector[:, 0], precision=highest) + jnp.einsum('fmc,mfn->cfn', kernel[1], vector[:, 1], precision=highest)
    imag_part = jnp.einsum('fmc,mfn->cfn', kernel[0], vector[:, 1], precision=highest) - jnp.einsum('fmc,mfn->cfn', kernel[1], vector[:, 0], precision=highest)
    return jnp.stack([real_part, imag_part], axis=1)

def rms_norm(vector):
    return jnp.sqrt(lax.optimization_barrier(jnp.sum(vector * vector, axis=(0, 1, 3))) / (2.0 * NR * SOURCES))

def widen(values):
    return values[None, None, :, None]

def reference(kernel, traces, acq_lists, counts):
    slot_index = jnp.arange(AREAS * CAP, dtype=jnp.int32)
    block_index = slot_index // CAP
    filled = (slot_index % CAP)[None, :] < counts[:, block_index]
    list_index = jnp.arange(LISTS, dtype=jnp.int32)[:, None]
    target = (acq_lists // ROWS * LISTS + list_index) * ROWS + acq_lists % ROWS
    target = jnp.where(filled, target, NR).astype(jnp.int32)
    observed = jnp.zeros((NR + 1, 2, FREQS, SOURCES), jnp.float32)
    observed = observed.at[target.reshape(-1)].add(traces.reshape(-1, 2, FREQS, SOURCES))[:NR]
    beta_norm = rms_norm(observed)
    left_unit = observed / widen(beta_norm)
    right_vec = kernel_adjoint(kernel, left_unit)
    alpha_norm = rms_norm(right_vec)
    right_unit = right_vec / widen(alpha_norm)
    search = right_unit
    solution = jnp.zeros((NR, 2, FREQS, SOURCES), jnp.float32)
    phibar = beta_norm
    rhobar = alpha_norm
    next_left = observed
    for iteration in range(ITERS):
        next_left = kernel_apply(kernel, right_unit) - widen(alpha_norm) * left_unit
        beta_norm = rms_norm(next_left)
        left_unit = next_left / widen(beta_norm)
        rho_value = jnp.sqrt(rhobar * rhobar + beta_norm * beta_norm)
        cosine = rhobar / rho_value
        sine_value = beta_norm / rho_value
        phi_value = cosine * phibar
        phibar = sine_value * phibar
        solution = solution + widen(phi_value / rho_value) * search
        if iteration + 1 < ITERS:
            right_vec = kernel_adjoint(kernel, left_unit) - widen(beta_norm) * right_unit
            alpha_norm = rms_norm(right_vec)
            right_unit = right_vec / widen(alpha_norm)
            theta_value = sine_value * alpha_norm
            rhobar = -cosine * alpha_norm
            search = right_unit - widen(theta_value / rho_value) * search
    return (solution, next_left)
```

```python
import functools
import jax
import jax.numpy as jnp
from jax import lax
from jax.experimental import pallas as pl
from jax.experimental.pallas import tpu as pltpu
from jax.sharding import PartitionSpec as P

NR = 5120
FREQS = 2
SOURCES = 256
ITERS = 2
NZ, NY, NX = 8, 4, 4
ROWS = 20
LANES = 512
BLK = 40
ROWS_REC = 160
COLS = 1280
MESH = pltpu.DeviceIdType.MESH if hasattr(pltpu, "DeviceIdType") else pl.DeviceIdType.MESH
F32 = jnp.float32
BF16 = jnp.bfloat16
COUNT = 2.0 * NR * SOURCES

ROWS_A = (0, 16)
ROWS_B = (16, 24)


class Copies:
    def __init__(self):
        self.names = {}

    def number(self, name):
        return self.names.setdefault(name, len(self.names))


def kernel_body(copies, k_hbm, traces, meta, sol_out, left_out, *scratch):
    (kf, s3, sp, kt3, p, vall, vh, vl, wst, uall, q, tbuf, mbuf, send_e, recv_e1, send_e2, recv_e2,
     rza, ryb, rzb, rya, rxq, nown, nx, ny, nz, left, vprev, wvec, sol, scal,
     ostage, orecv, ssem, rsem, lsem) = scratch
    r = lax.axis_index("rec")
    s = lax.axis_index("src")
    z, y = r // NY, r % NY
    x, c = s // 2, s % 2
    oc = 1 - c

    def dev(dz=0, dy=0, dx=0, flip=False):
        zz = lax.rem(z + dz + 2 * NZ, NZ)
        yy = lax.rem(y + dy + 2 * NY, NY)
        xx = lax.rem(x + dx + 2 * NX, NX)
        return (zz * NY + yy, xx * 2 + (oc if flip else c))

    def zat(d):
        return lax.rem(z + d + 2 * NZ, NZ)

    def yat(d):
        return lax.rem(y + d + 2 * NY, NY)

    def xat(d):
        return lax.rem(x + d + 2 * NX, NX)

    pending = []

    def send(name, src, dst, target):
        i = copies.number(name)
        copy = pltpu.make_async_remote_copy(
            src_ref=src, dst_ref=dst, send_sem=ssem.at[i], recv_sem=rsem.at[i],
            device_id=target, device_id_type=MESH)
        copy.start()
        pending.append(copy)

    def recv(name, dst):
        i = copies.number(name)
        pltpu.make_async_remote_copy(
            src_ref=dst, dst_ref=dst, send_sem=ssem.at[i], recv_sem=rsem.at[i],
            device_id=dev(flip=True), device_id_type=MESH).wait_recv()

    def flush():
        for copy in pending:
            copy.wait_send()
        pending.clear()

    own_k = pltpu.make_async_copy(k_hbm.at[:, c], kf.at[:, c], lsem.at[0])
    own_k.start()
    own_t = pltpu.make_async_copy(traces.at[c], tbuf.at[pl.ds(c * 32, 32)], lsem.at[1])
    own_t.start()
    barrier = pltpu.get_barrier_semaphore()
    friends = [dev(dz=d) for d in range(1, NZ)] + [dev(dy=d) for d in range(1, NY)]
    friends += [dev(dx=d) for d in range(1, NX)] + [dev(flip=True)]
    for friend in friends:
        pl.semaphore_signal(barrier, inc=1, device_id=friend, device_id_type=MESH)
    pl.semaphore_wait(barrier, len(friends))

    send("meta", meta, mbuf, dev(flip=True))
    send("traces", traces.at[oc], tbuf.at[pl.ds(c * 32, 32)], dev(flip=True))
    send("k", k_hbm.at[:, oc], kf.at[:, c], dev(flip=True))

    own_t.wait()
    recv("meta", mbuf)
    recv("traces", tbuf.at[pl.ds(oc * 32, 32)])
    ids = jnp.maximum(meta[0:1, :], mbuf[0:1, :])
    row = lax.broadcasted_iota(jnp.int32, (64, 128), 0)
    lane = lax.broadcasted_iota(jnp.int32, (64, 128), 1)
    area = (row >> 3) * NY + (row & 3)
    offset = ids - ROWS * area
    match = (offset >= 0) & (offset < ROWS) & ((lane >> 5) == ((row >> 2) & 1))
    picked = jnp.dot(jnp.where(match, 1.0, 0.0)[:, :64], tbuf[...],
                     preferred_element_type=F32, precision=lax.Precision.HIGHEST)
    place = jnp.sum(jnp.where(match, (offset + 1).astype(F32), 0.0), axis=1, keepdims=True)
    send_e[:, :, 0:LANES] = picked.reshape(NZ, 8, LANES)
    send_e[:, :, LANES:] = jnp.broadcast_to(place, (64, 128)).reshape(NZ, 8, 128)
    for d in (4, 3, 5, 2, 6, 1, 7):
        send(("e1", d), send_e.at[zat(d)], recv_e1.at[pl.ds(pl.multiple_of(z * 8, 8), 8)], dev(dz=d))
    recv_e1[pl.ds(pl.multiple_of(z * 8, 8), 8), :] = send_e[z]
    for d in (1, 7, 2, 6, 3, 5, 4):
        recv(("e1", d), recv_e1.at[pl.ds(pl.multiple_of(zat(-d) * 8, 8), 8)])
    swap = jnp.where(lane == (row & 15) * 4 + (row >> 4), 1.0, 0.0)[:, :64]
    send_e2[...] = jnp.dot(swap, recv_e1[...], preferred_element_type=F32,
                           precision=lax.Precision.HIGHEST).reshape(NY, 16, 640)
    for d in (2, 1, 3):
        send(("e2", d), send_e2.at[yat(d)], recv_e2.at[y], dev(dy=d))
    recv_e2[y] = send_e2[y]
    for d in (1, 3, 2):
        recv(("e2", d), recv_e2.at[yat(-d)])
    got = recv_e2[...].reshape(64, 640)
    slot = got[:, LANES:]
    wanted = slot - 1.0 + jnp.where((row & 1) == 1, float(ROWS), 0.0)
    onehot = jnp.where((slot > 0.5) & (lane.astype(F32) == wanted), 1.0, 0.0)
    left[...] = jnp.dot(jnp.transpose(onehot)[:BLK, :], got[:, :LANES],
                        preferred_element_type=F32, precision=lax.Precision.HIGHEST)

    own_k.wait()
    recv("k", kf.at[:, oc])
    for half in range(2):
        for part in range(2):
            cols = slice(half * 640, half * 640 + 640)
            value = kf[part, half]
            high = value.astype(BF16)
            low = (value - high.astype(F32)).astype(BF16)
            base = part * ROWS_REC
            s3[base:base + ROWS_REC, cols] = high
            s3[base + 320:base + 320 + ROWS_REC, cols] = low
            s3[base + 640:base + 640 + ROWS_REC, cols] = high

    def permute(i, carry):
        start = pl.multiple_of(i * 256, 256)
        new = lax.broadcasted_iota(jnp.int32, (256, COLS), 0) + start
        rec = (new * 1639) >> 16
        rest = new - rec * BLK
        second = rest >= ROWS
        old = jnp.where(second, 640 - ROWS, 0) + rec * ROWS + rest
        pick = jnp.where(lax.broadcasted_iota(jnp.int32, (256, COLS), 1) == old, 1.0, 0.0).astype(BF16)
        dims = (((1,), (1,)), ((), ()))
        sp[:, pl.ds(start, 256)] = lax.dot_general(
            s3[0:640, :], pick, dims, preferred_element_type=F32).astype(BF16)
        kt3[pl.ds(start, 256), :] = lax.dot_general(
            pick, s3[...], dims, preferred_element_type=F32).astype(BF16)
        return carry

    lax.fori_loop(0, COLS // 256, permute, 0)
    flush()

    def squares(value):
        squared = value * value
        total = squared[0:8, 0:128]
        for a in range(BLK // 8):
            for b in range(LANES // 128):
                if a or b:
                    total = total + squared[a * 8:a * 8 + 8, b * 128:b * 128 + 128]
        return total

    def norm_send(kind, axis, tile):
        size, buf, at, me = {"x": (NX, nx, xat, x), "y": (NY, ny, yat, y), "z": (NZ, nz, zat, z)}[axis]
        stage = {"x": 0, "y": 1, "z": 2}[axis]
        nown[kind, stage] = tile
        buf[kind, me] = tile
        for d in sorted(range(1, size), key=lambda d: -min(d, size - d)):
            send(("n", kind, axis, d), nown.at[kind, stage], buf.at[kind, me], dev(**{"d" + axis: d}))

    def norm_recv(kind, axis):
        size, buf, at = {"x": (NX, nx, xat), "y": (NY, ny, yat), "z": (NZ, nz, zat)}[axis]
        for d in range(1, size):
            recv(("n", kind, axis, d), buf.at[kind, at(-d)])
        total = buf[kind, 0]
        for i in range(1, size):
            total = total + buf[kind, i]
        return total

    def root(tile):
        return jnp.sqrt(jnp.sum(tile, axis=(0, 1), keepdims=True) / COUNT)

    HALF_A = {1: pl.ds(0, 8), -1: pl.ds(8, 8)}
    ALL_A = pl.ds(0, 16)
    ALL_B = pl.ds(16, 24)

    def half_b(parity, way):
        if (parity % 2 == 0) == (way == 1):
            return pl.ds(16, 16)
        return pl.ds(32, 8)

    def size_of(ds):
        return ds.size

    def gather_x():
        for way in (1, -1):
            send(("gx", way, 1), uall.at[x], uall.at[x], dev(dx=way))
        for way in (1, -1):
            recv(("gx", way, 1), uall.at[xat(-way)])
            rows = pl.ds(0, 16) if way == 1 else pl.ds(16, 24)
            send(("gx", way, 2), uall.at[xat(-way), rows], uall.at[xat(-way), rows], dev(dx=way))
        for way in (1, -1):
            rows = pl.ds(0, 16) if way == 1 else pl.ds(16, 24)
            recv(("gx", way, 2), uall.at[xat(-2), rows])

    def scatter_x():
        for way in (1, -1):
            rows = pl.ds(0, 16) if way == 1 else pl.ds(16, 24)
            send(("sx", way, 1), q.at[xat(2), rows], rxq.at[0 if way == 1 else 1, 0, rows], dev(dx=way))
        for way in (1, -1):
            i = 0 if way == 1 else 1
            rows = pl.ds(0, 16) if way == 1 else pl.ds(16, 24)
            recv(("sx", way, 1), rxq.at[i, 0, rows])
            q[xat(way), rows] += rxq[i, 0, rows]
            send(("sx", way, 2), q.at[xat(way)], rxq.at[i, 1], dev(dx=way))
        for way in (1, -1):
            recv(("sx", way, 2), rxq.at[0 if way == 1 else 1, 1])
        return q[x] + rxq[0, 1] + rxq[1, 1]

    WAYS = (1, -1)

    def wi(way):
        return 0 if way == 1 else 1

    def za_rows(way, t):
        return HALF_A[way] if t == 1 else ALL_A

    def za_send(way, t, g):
        rows = za_rows(way, t)
        block = p.at[zat(way * (5 - t)), pl.ds(2 * g, 2), rows]
        send(("za", way, t, g), block, rza.at[wi(way), t - 1, g, :, pl.ds(0, size_of(rows))], dev(dz=way))

    def za_recv(way, t, g):
        rows = za_rows(way, t)
        n = size_of(rows)
        recv(("za", way, t, g), rza.at[wi(way), t - 1, g, :, pl.ds(0, n)])
        p[zat(way * (4 - t)), pl.ds(2 * g, 2), rows] += rza[wi(way), t - 1, g, :, pl.ds(0, n)]

    def yb_rows(d, way, t):
        return half_b(d, way) if t == 1 else ALL_B

    def yb_send(d, way, t):
        rows = yb_rows(d, way, t)
        block = p.at[zat(d), yat(way * (3 - t)), rows]
        send(("yb", d, way, t), block, ryb.at[d, wi(way), t - 1, pl.ds(0, size_of(rows))], dev(dy=way))

    def yb_recv(d, way, t):
        rows = yb_rows(d, way, t)
        n = size_of(rows)
        recv(("yb", d, way, t), ryb.at[d, wi(way), t - 1, pl.ds(0, n)])
        p[zat(d), yat(way * (2 - t)), rows] += ryb[d, wi(way), t - 1, pl.ds(0, n)]

    def zb_rows(way, t):
        return half_b(0, way) if t == 1 else ALL_B

    def zb_send(way, t):
        rows = zb_rows(way, t)
        block = p.at[zat(way * (5 - t)), y, rows]
        send(("zb", way, t), block, rzb.at[wi(way), t - 1, pl.ds(0, size_of(rows))], dev(dz=way))

    def zb_recv(way, t):
        rows = zb_rows(way, t)
        n = size_of(rows)
        recv(("zb", way, t), rzb.at[wi(way), t - 1, pl.ds(0, n)])
        p[zat(way * (4 - t)), y, rows] += rzb[wi(way), t - 1, pl.ds(0, n)]

    def ya_send(way, t):
        rows = HALF_A[way] if t == 1 else ALL_A
        block = p.at[z, yat(way * (3 - t)), rows]
        send(("ya", way, t), block, rya.at[wi(way), t - 1, pl.ds(0, size_of(rows))], dev(dy=way))

    def ya_recv(way, t):
        rows = HALF_A[way] if t == 1 else ALL_A
        n = size_of(rows)
        recv(("ya", way, t), rya.at[wi(way), t - 1, pl.ds(0, n)])
        p[z, yat(way * (2 - t)), rows] += rya[wi(way), t - 1, pl.ds(0, n)]

    def scatter_rec(between_one, between_two):
        order = (4, 3, 5, 2, 6, 1, 7, 0)
        for g in range(2):
            for way in WAYS:
                za_send(way, 1, g)
        for d in order:
            for way in WAYS:
                yb_send(d, way, 1)

        def yb_mid(d):
            for way in WAYS:
                yb_recv(d, way, 1)
                yb_send(d, way, 2)

        def yb_end(d):
            for way in WAYS:
                yb_recv(d, way, 2)

        def za_step(t):
            for g in range(2):
                for way in WAYS:
                    za_recv(way, t, g)
                    if t < 4:
                        za_send(way, t + 1, g)

        def zb_step(t):
            for way in WAYS:
                zb_recv(way, t)
                if t < 4:
                    zb_send(way, t + 1)

        def ya_start():
            for way in WAYS:
                ya_send(way, 1)

        yb_mid(4)
        between_one()
        za_step(1)
        yb_mid(3)
        yb_mid(5)
        za_step(2)
        yb_end(4)
        for way in WAYS:
            zb_send(way, 1)
        yb_mid(2)
        yb_mid(6)
        between_two()
        za_step(3)
        yb_end(3)
        yb_end(5)
        zb_step(1)
        yb_mid(1)
        yb_mid(7)
        za_step(4)
        ya_start()
        yb_end(2)
        yb_end(6)
        zb_step(2)
        yb_mid(0)
        for way in WAYS:
            ya_recv(way, 1)
            ya_send(way, 2)
        yb_end(1)
        yb_end(7)
        zb_step(3)
        yb_end(0)
        for way in WAYS:
            ya_recv(way, 2)
        zb_step(4)
        return p[z, y]

    def gather_rec(between):
        def bz_rows(way, t):
            return half_b(0, way) if t == 4 else ALL_B

        def bz_send(way, t):
            rows = bz_rows(way, t)
            block = vall.at[zat(-way * (t - 1)), y, rows]
            send(("bz", way, t), block, block, dev(dz=way))

        def bz_recv(way, t):
            recv(("bz", way, t), vall.at[zat(-way * t), y, bz_rows(way, t)])

        def by_rows(d, way, t):
            return half_b(d, way) if t == 2 else ALL_B

        def by_send(d, way, t):
            block = vall.at[zat(d), yat(-way * (t - 1)), by_rows(d, way, t)]
            send(("by", d, way, t), block, block, dev(dy=way))

        def by_recv(d, way, t):
            recv(("by", d, way, t), vall.at[zat(d), yat(-way * t), by_rows(d, way, t)])

        def ay_send(way, t):
            block = vall.at[z, yat(-way * (t - 1)), HALF_A[way] if t == 2 else ALL_A]
            send(("ay", way, t), block, block, dev(dy=way))

        def ay_recv(way, t):
            recv(("ay", way, t), vall.at[z, yat(-way * t), HALF_A[way] if t == 2 else ALL_A])

        def az_rows(way, t):
            return HALF_A[way] if t == 4 else ALL_A

        def az_send(way, t, g):
            block = vall.at[zat(-way * (t - 1)), pl.ds(2 * g, 2), az_rows(way, t)]
            send(("az", way, t, g), block, block, dev(dz=way))

        def az_recv(way, t, g):
            recv(("az", way, t, g), vall.at[zat(-way * t), pl.ds(2 * g, 2), az_rows(way, t)])

        def by_start(d):
            for way in WAYS:
                by_send(d, way, 1)

        def by_mid(d):
            for way in WAYS:
                by_recv(d, way, 1)
                by_send(d, way, 2)

        def bz_step(t):
            for way in WAYS:
                bz_recv(way, t)
                if t < 4:
                    bz_send(way, t + 1)
            if t < 4:
                by_start(t)
                by_start(8 - t)
            else:
                by_start(4)

        def az_step(t):
            for g in range(2):
                for way in WAYS:
                    az_recv(way, t, g)
                    if t < 4:
                        az_send(way, t + 1, g)

        for way in WAYS:
            ay_send(way, 1)
            bz_send(way, 1)
        by_start(0)
        for way in WAYS:
            ay_recv(way, 1)
            ay_send(way, 2)
        bz_step(1)
        for way in WAYS:
            ay_recv(way, 2)
        for g in range(2):
            for way in WAYS:
                az_send(way, 1, g)
        by_mid(0)
        bz_step(2)
        between()
        by_mid(1)
        by_mid(7)
        az_step(1)
        bz_step(3)
        by_mid(2)
        by_mid(6)
        bz_step(4)
        az_step(2)
        by_mid(3)
        by_mid(5)
        az_step(3)
        by_mid(4)
        for d in (0, 1, 7, 2, 6, 3, 5, 4):
            for way in WAYS:
                by_recv(d, way, 2)
        az_step(4)

    def adjoint_products():
        value = uall[...].reshape(ROWS_REC, LANES)
        real, imag = value[:, :SOURCES], value[:, SOURCES:]
        for base, both in ((0, (real, imag)), (ROWS_REC, (imag, -real))):
            for i in range(2):
                cols = slice(i * SOURCES, i * SOURCES + SOURCES)
                high = both[i].astype(BF16)
                wst[base:base + ROWS_REC, cols] = high
                wst[base + 320:base + 320 + ROWS_REC, cols] = high
                wst[base + 640:base + 640 + ROWS_REC, cols] = (both[i] - high.astype(F32)).astype(BF16)

        def tile(i, carry):
            start = pl.multiple_of(i * 320, 320)
            out = jnp.dot(kt3[pl.ds(start, 320), :], wst[...], preferred_element_type=F32)
            p[pl.ds(i * 2, 2)] = out.reshape(2, NY, BLK, LANES)
            return carry

        lax.fori_loop(0, 4, tile, 0)

    def forward_products():
        def parts(i, carry):
            value = vall[i].reshape(NY * BLK, LANES)
            high = value.astype(BF16)
            rows = pl.ds(pl.multiple_of(i * 160, 160), 160)
            vh[rows, :] = high
            vl[rows, :] = (value - high.astype(F32)).astype(BF16)
            return carry

        lax.fori_loop(0, NZ, parts, 0)
        outs = []
        for i in range(2):
            cols = slice(i * SOURCES, i * SOURCES + SOURCES)
            one = jnp.dot(sp[...], vh[:, cols], preferred_element_type=F32)
            two = jnp.dot(sp[0:320, :], vl[:, cols], preferred_element_type=F32)
            outs.append(one[0:320] + one[320:640] + two)
        real = outs[0][:ROWS_REC] - outs[1][ROWS_REC:]
        imag = outs[1][:ROWS_REC] + outs[0][ROWS_REC:]
        q[:, :, :SOURCES] = real.reshape(NX, BLK, SOURCES)
        q[:, :, SOURCES:] = imag.reshape(NX, BLK, SOURCES)

    vprev[...] = jnp.zeros_like(vprev)
    wvec[...] = jnp.zeros_like(wvec)
    sol[...] = jnp.zeros_like(sol)
    scal[...] = jnp.ones_like(scal)

    def iteration(it, carry):
        first = it == 0
        left_now = left[...]
        uall[x] = left_now
        norm_send(0, "x", squares(left_now))
        gather_x()
        adjoint_products()
        norm_send(0, "y", norm_recv(0, "x"))
        box = {}

        def one():
            norm_send(0, "z", norm_recv(0, "y"))

        def two():
            box["beta"] = root(norm_recv(0, "z"))

        summed = scatter_rec(one, two)
        flush()
        beta = box["beta"]
        alpha_old = scal[0, 0:1, 0:1]
        phibar_old = scal[1, 0:1, 0:1]
        rhobar_old = scal[2, 0:1, 0:1]
        right = summed / beta - beta * vprev[...]
        vall[z, y] = right
        norm_send(1, "y", squares(right))

        def three():
            norm_send(1, "z", norm_recv(1, "y"))

        gather_rec(three)
        rho = jnp.sqrt(rhobar_old * rhobar_old + beta * beta)
        cosine = rhobar_old / rho
        sine = beta / rho
        phi = cosine * phibar_old
        wold = wvec[...]
        sol[...] += jnp.where(first, 0.0, phi / rho) * wold
        forward_products()
        norm_send(1, "x", norm_recv(1, "z"))
        product = scatter_x()
        alpha = root(norm_recv(1, "x"))
        vnew = vall[z, y] / alpha
        theta = sine * alpha
        wvec[...] = vnew - jnp.where(first, 0.0, theta / rho) * wold
        vprev[...] = vnew
        next_left = product / alpha - alpha * (left_now / beta)
        left[...] = next_left
        scal[0] = jnp.broadcast_to(alpha, (8, 128))
        scal[1] = jnp.broadcast_to(jnp.where(first, beta, sine * phibar_old), (8, 128))
        scal[2] = jnp.broadcast_to(jnp.where(first, alpha, -cosine * alpha), (8, 128))
        flush()
        return carry

    lax.fori_loop(0, ITERS, iteration, 0)

    last = left[...]
    norm_send(2, "x", squares(last))

    def stage(i, value):
        ostage[i, 0, 0:ROWS] = value[:ROWS]
        ostage[i, 1, 0:ROWS] = value[ROWS:]

    stage(0, last)
    send(("out", 0), ostage.at[0, oc], orecv.at[0], dev(flip=True))
    norm_send(2, "y", norm_recv(2, "x"))
    norm_send(2, "z", norm_recv(2, "y"))
    beta = root(norm_recv(2, "z"))
    phibar = scal[1, 0:1, 0:1]
    rhobar = scal[2, 0:1, 0:1]
    rho = jnp.sqrt(rhobar * rhobar + beta * beta)
    phi = (rhobar / rho) * phibar
    stage(1, sol[...] + (phi / rho) * wvec[...])
    send(("out", 1), ostage.at[1, oc], orecv.at[1], dev(flip=True))

    for i, out in ((0, left_out), (1, sol_out)):
        recv(("out", i), orecv.at[i])
        mine = ostage[i, c, 0:ROWS]
        other = orecv[i, 0:ROWS]
        slab0 = jnp.where(c == 0, mine, other)
        slab1 = jnp.where(c == 0, other, mine)
        out[:, 0:256] = slab0[:, :SOURCES]
        out[:, 256:512] = slab1[:, :SOURCES]
        out[:, 512:768] = slab0[:, SOURCES:]
        out[:, 768:1024] = slab1[:, SOURCES:]
    flush()


COPIES = 320


def on_device(kernel, traces, acq_lists, counts):
    core = lax.axis_index("src") % 2
    slots = traces.shape[1]
    by_slab = jnp.transpose(traces[0], (2, 0, 1, 3)).reshape(FREQS, slots, LANES)
    by_slab = jnp.pad(by_slab, ((0, 0), (0, 32 - slots), (0, 0)))
    lane = jnp.arange(128, dtype=jnp.int32)
    padded = jnp.pad(acq_lists[0], (0, 32 - slots))
    inside = lane - core * 32
    used = (inside >= 0) & (inside < counts[0, 0])
    meta = jnp.where(used, jnp.tile(padded, 4), -1)
    meta = jnp.broadcast_to(meta[None, :], (8, 128)).astype(jnp.int32)
    vmem = pltpu.VMEM
    scratch = [
        vmem((2, 2, ROWS_REC, 640), F32),
        vmem((960, COLS), BF16),
        vmem((640, COLS), BF16),
        vmem((COLS, 960), BF16),
        vmem((NZ, NY, BLK, LANES), F32),
        vmem((NZ, NY, BLK, LANES), F32),
        vmem((COLS, LANES), BF16),
        vmem((COLS, LANES), BF16),
        vmem((960, LANES), BF16),
        vmem((NX, BLK, LANES), F32),
        vmem((NX, BLK, LANES), F32),
        vmem((64, LANES), F32),
        vmem((8, 128), jnp.int32),
        vmem((NZ, 8, 640), F32),
        vmem((64, 640), F32),
        vmem((NY, 16, 640), F32),
        vmem((NY, 16, 640), F32),
        vmem((2, 4, 2, 2, 16, LANES), F32),
        vmem((8, 2, 2, 24, LANES), F32),
        vmem((2, 4, 24, LANES), F32),
        vmem((2, 2, 16, LANES), F32),
        vmem((2, 2, BLK, LANES), F32),
        vmem((3, 3, 8, 128), F32),
        vmem((3, NX, 8, 128), F32),
        vmem((3, NY, 8, 128), F32),
        vmem((3, NZ, 8, 128), F32),
        vmem((BLK, LANES), F32),
        vmem((BLK, LANES), F32),
        vmem((BLK, LANES), F32),
        vmem((BLK, LANES), F32),
        vmem((3, 8, 128), F32),
        vmem((2, 2, 24, LANES), F32),
        vmem((2, 24, LANES), F32),
        pltpu.SemaphoreType.DMA((COPIES,)),
        pltpu.SemaphoreType.DMA((COPIES,)),
        pltpu.SemaphoreType.DMA((2,)),
    ]
    whole = pl.BlockSpec(memory_space=pltpu.VMEM)
    outs = pl.pallas_call(
        functools.partial(kernel_body, Copies()),
        out_shape=(jax.ShapeDtypeStruct((ROWS, 1024), F32),) * 2,
        in_specs=[pl.BlockSpec(memory_space=pl.ANY), whole, whole],
        out_specs=(whole, whole),
        scratch_shapes=scratch,
        compiler_params=pltpu.CompilerParams(
            collective_id=0, has_side_effects=True, vmem_limit_bytes=60 * 1024 * 1024),
    )(kernel, by_slab, meta)
    return tuple(out.reshape(ROWS, 2, FREQS, SOURCES) for out in outs)


def solution(mesh):
    placed = (
        P(None, None, "rec", "src"),
        P("src", "rec", None, None, None),
        P("src", "rec"),
        P("src", "rec"),
    )
    return jax.shard_map(
        on_device,
        mesh=mesh,
        in_specs=placed,
        out_specs=(P(("src", "rec"), None, None, None), P(("rec", "src"), None, None, None)),
        check_vma=False,
    )
```

```python
import functools
import jax
import jax.numpy as jnp
from jax import lax
from jax.experimental import pallas as pl
from jax.experimental.pallas import tpu as pltpu
from jax.sharding import PartitionSpec as P

NR = 5120
FREQS = 2
SOURCES = 256
ITERS = 2
NZ, NY, NX = 8, 4, 4
SIZE = {"x": NX, "y": NY, "z": NZ}
ROWS = 20
HALVES = 2
WIDE = SOURCES // HALVES
LANES = 2 * WIDE
BLK = 40
ROWS_REC = 160
COLS = 1280
COPIES = 80
GROUPS = 16
AHEAD = 4
MESH = pl.DeviceIdType.MESH
F32 = jnp.float32
BF16 = jnp.bfloat16
COUNT = 2.0 * NR * SOURCES
EXACT = lax.Precision.HIGHEST
NEVER = 1e9

RATE = 51e3
RATE_CHIP = 600e3
DELAY = {("c", 0): 0.9, ("z", 1): 2.5, ("z", 2): 3.1, ("z", 3): 3.7, ("z", 4): 4.3}
DELAY.update({(a, d): 2.8 + 0.2 * d for a in "xy" for d in (1, 2)})
WAYS = (1, -1)


class Plan:
    def __init__(self):
        self.now = 0.0
        self.link = {}
        self.arrived = {}
        self.counted = {}
        self.expected = {}
        self.events = {}
        self.numbers = {}
        self.tasks = []
        self.log = []

    def number(self, name):
        return self.numbers.setdefault(name, len(self.numbers))

    def add(self, task, rank=0):
        self.tasks.append([rank, len(self.log), task, None])
        self.log.append(rank)
        self.step(self.tasks[-1])

    def sent(self, key, axis, d, size):
        hops = min(d % SIZE[axis], -d % SIZE[axis]) if axis != "c" else 0
        if axis == "c":
            paths, load = [axis], size / RATE_CHIP
        elif 2 * hops == SIZE[axis]:
            paths, load = [(axis, 1), (axis, -1)], size * hops / 2 / RATE
        else:
            paths, load = [(axis, 1 if d % SIZE[axis] == hops else -1)], size * hops / RATE
        start = max([self.now] + [self.link.get(path, 0.0) for path in paths])
        for path in paths:
            self.link[path] = start + load
        came = start + load + DELAY[axis, hops]
        self.arrived[key] = max(self.arrived.get(key, 0.0), came)
        self.counted[key] = self.counted.get(key, 0) + size

    def mark(self, name):
        self.events[name] = self.now

    def ready(self, need):
        if need is None:
            return 0.0
        if need[0] == "r":
            if self.counted.get(need[1], 0) < need[2]:
                return NEVER
            return self.arrived[need[1]]
        return max(self.events.get(name, NEVER) for name in need[1])

    def step(self, entry):
        try:
            entry[3] = next(entry[2])
        except StopIteration:
            self.tasks.remove(entry)

    def run(self):
        while self.tasks:
            times = [self.ready(entry[3]) for entry in self.tasks]
            first = min(times)
            if first >= NEVER:
                raise ValueError("stuck")
            self.now = max(self.now, first)
            able = [e for e, t in zip(self.tasks, times) if t <= self.now]
            best = min(able, key=lambda e: (e[0], self.ready(e[3]), e[1]))
            self.step(best)


def rows_a(way, part):
    return pl.ds(0 if way == 1 else 8, 8) if part else pl.ds(0, 16)


def rows_b(way, part):
    if not part:
        return pl.ds(16, 24)
    return pl.ds(16, 16) if way == 1 else pl.ds(32, 8)


def ii(way):
    return 0 if way == 1 else 1


def kernel_body(k_hbm, traces, ids_ref, counts_ref, sol_out, left_out, *scratch):
    (kf, s3, sp, kt3, pick, p, vall, vh, vl, wst, uall, q, acc, tbuf, tsend, meta, mbuf,
     send_e, recv_e1, send_e2, recv_e2, rza1, rza2, ryb, rzb1, rzb2, rya, rxq, dummy, nown, nx, ny, nz,
     left, ostage, orecv, ssem, rsem, lsem) = scratch
    plan = Plan()
    r = lax.axis_index("rec")
    s = lax.axis_index("src")
    z, y = r // NY, r % NY
    x, c = s // 2, s % 2
    oc = 1 - c
    me = {"x": x, "y": y, "z": z}

    def at(axis, d):
        return lax.rem(me[axis] + d + 2 * SIZE[axis], SIZE[axis])

    def dev(axis, d):
        zz = at("z", d) if axis == "z" else z
        yy = at("y", d) if axis == "y" else y
        xx = at("x", d) if axis == "x" else x
        return (zz * NY + yy, xx * 2 + (oc if axis == "c" else c))

    pending = {}
    groups = {}

    def size_of(ref):
        size = 4
        for n in ref.shape:
            size *= n
        return size

    def waiting(size, i, sems):
        rows = dummy.at[pl.ds(0, size // 512)]
        return pltpu.make_async_copy(rows, rows, sems.at[i])

    def send(it, name, src, dst, axis, d, group):
        i = plan.number(name)
        g = groups.setdefault(group, len(groups))
        pltpu.make_async_remote_copy(
            src_ref=src, dst_ref=dst, send_sem=ssem.at[g], recv_sem=rsem.at[i],
            device_id=dev(axis, d), device_id_type=MESH).start()
        pending[group] = pending.get(group, 0) + size_of(src)
        plan.sent((it, name), axis, d, size_of(src))

    def wait_recv(it, name, size):
        yield ("r", (it, name), size)
        waiting(size, plan.number(name), rsem).wait()

    def flush(*names):
        for group in names:
            size = pending.pop(group, 0)
            if size:
                waiting(size, groups[group], ssem).wait()

    def need(*names):
        return ("e", names)

    def spend(us):
        plan.now += us

    own_k = pltpu.make_async_copy(k_hbm.at[:, c], kf.at[:, c], lsem.at[0])
    own_k.start()
    barrier = pltpu.get_barrier_semaphore()
    friends = [(a, d) for a in ("z", "y", "x") for d in range(1, SIZE[a])] + [("c", 0)]
    for friend in friends:
        pl.semaphore_signal(barrier, inc=1, device_id=dev(*friend), device_id_type=MESH)

    slots = traces.shape[1]
    lane_row = lax.broadcasted_iota(jnp.int32, (1, slots), 1)
    listed = jnp.where(lane_row < counts_ref[...], ids_ref[...], -1)
    meta[...] = jnp.full((8, 128), -1, jnp.int32)

    @pl.when(c == 0)
    def _():
        meta[0:1, 0:slots] = listed

    @pl.when(c == 1)
    def _():
        meta[0:1, 32:32 + slots] = listed

    blank = jnp.zeros((32, HALVES * LANES), F32)
    tbuf[pl.ds(pl.multiple_of(c * 32, 32), 32), :] = blank
    tsend[...] = blank
    for half in range(HALVES):
        for part in range(2):
            cols = slice(half * LANES + part * WIDE, half * LANES + part * WIDE + WIDE)
            lanes = slice(half * WIDE, half * WIDE + WIDE)
            slab0 = traces[0, :, part, 0, lanes]
            slab1 = traces[0, :, part, 1, lanes]
            tsend[0:slots, cols] = jnp.where(c == 0, slab1, slab0)
            tbuf[pl.ds(pl.multiple_of(c * 32, 32), slots), cols] = jnp.where(c == 0, slab0, slab1)
    pl.semaphore_wait(barrier, len(friends))
    send(0, "meta", meta, mbuf, "c", 0, "in")
    send(0, "traces", tsend, tbuf.at[pl.ds(c * 32, 32)], "c", 0, "in")
    send(0, "k", k_hbm.at[:, oc], kf.at[:, c], "c", 0, "in")

    row = lax.broadcasted_iota(jnp.int32, (64, 128), 0)
    lane = lax.broadcasted_iota(jnp.int32, (64, 128), 1)
    wide = HALVES * LANES

    def observe():
        yield from wait_recv(0, "meta", 4096)
        yield from wait_recv(0, "traces", size_of(tsend))
        ids = jnp.maximum(meta[0:1, :], mbuf[0:1, :])
        area = (row >> 3) * NY + (row & 3)
        offset = ids - ROWS * area
        match = (offset >= 0) & (offset < ROWS) & ((lane >> 5) == ((row >> 2) & 1))
        picked = jnp.dot(jnp.where(match, 1.0, 0.0)[:, :64], tbuf[...],
                         preferred_element_type=F32, precision=EXACT)
        place = jnp.sum(jnp.where(match, (offset + 1).astype(F32), 0.0), axis=1, keepdims=True)
        send_e[:, :, 0:wide] = picked.reshape(NZ, 8, wide)
        send_e[:, :, wide:] = jnp.broadcast_to(place, (64, 128)).reshape(NZ, 8, 128)
        spend(0.8)
        mine = pl.ds(pl.multiple_of(z * 8, 8), 8)
        for d in (4, 3, 5, 2, 6, 1, 7):
            send(0, "e1", send_e.at[at("z", d)], recv_e1.at[mine], "z", d, "in")
        recv_e1[mine, :] = send_e[z]
        yield from wait_recv(0, "e1", 7 * size_of(send_e.at[0]))
        swap = jnp.where(lane == (row & 15) * 4 + (row >> 4), 1.0, 0.0)[:, :64]
        send_e2[...] = jnp.dot(swap, recv_e1[...], preferred_element_type=F32,
                               precision=EXACT).reshape(NY, 16, wide + 128)
        spend(0.8)
        for d in (2, 1, 3):
            send(0, "e2", send_e2.at[at("y", d)], recv_e2.at[y], "y", d, "in")
        recv_e2[y] = send_e2[y]
        yield from wait_recv(0, "e2", 3 * size_of(send_e2.at[0]))
        got = recv_e2[...].reshape(64, wide + 128)
        slot = got[:, wide:]
        wanted = slot - 1.0 + jnp.where((row & 1) == 1, float(ROWS), 0.0)
        onehot = jnp.where((slot > 0.5) & (lane.astype(F32) == wanted), 1.0, 0.0)
        value = jnp.dot(jnp.transpose(onehot)[:BLK, :], got[:, :wide],
                        preferred_element_type=F32, precision=EXACT)
        spend(0.8)
        for h in range(HALVES):
            left[h] = value[:, h * LANES:h * LANES + LANES]
            plan.mark(("left", 0, h))

    def split_half(half):
        for part in range(2):
            cols = pl.ds(pl.multiple_of(half * 640, 128), 640)
            value = kf[part, half]
            high = value.astype(BF16)
            low = (value - high.astype(F32)).astype(BF16)
            base = part * ROWS_REC
            s3[base:base + ROWS_REC, cols] = high
            s3[base + 320:base + 320 + ROWS_REC, cols] = low
            s3[base + 640:base + 640 + ROWS_REC, cols] = high

    dims = (((1,), (1,)), ((), ()))

    def order_kernel():
        def build(i, carry):
            start = pl.multiple_of(i * 256, 256)
            new = lax.broadcasted_iota(jnp.int32, (256, 128), 0) + start
            rec = (new * 1639) >> 16
            rest = new - rec * BLK
            old = jnp.where(rest >= ROWS, 640 - ROWS, 0) + rec * ROWS + rest
            lanes = lax.broadcasted_iota(jnp.int32, (256, 128), 1)
            for j in range(COLS // 128):
                pick[pl.ds(start, 256), j * 128:j * 128 + 128] = jnp.where(
                    lanes + j * 128 == old, 1.0, 0.0).astype(BF16)
            return carry

        lax.fori_loop(0, COLS // 256, build, 0)
        spend(1.5)
        own_k.wait()
        split_half(c)
        spend(0.4)
        yield from wait_recv(0, "k", size_of(kf.at[:, 0]))
        split_half(oc)
        spend(0.4)

        def turned(i, carry):
            start = pl.multiple_of(i * 256, 256)
            kt3[pl.ds(start, 256), :] = lax.dot_general(
                pick[pl.ds(start, 256), :], s3[...], dims, preferred_element_type=F32).astype(BF16)
            return carry

        lax.fori_loop(0, COLS // 256, turned, 0)
        spend(3.0)
        plan.mark("kt3")
        yield need(("left", 0, 0))

        def straight(i, carry):
            start = pl.multiple_of(i * 256, 256)
            sp[:, pl.ds(start, 256)] = lax.dot_general(
                s3[0:640, :], pick[pl.ds(start, 256), :], dims, preferred_element_type=F32).astype(BF16)
            return carry

        yield need(("gx", 0, HALVES - 1))
        lax.fori_loop(0, COLS // 256, straight, 0)
        spend(2.5)
        plan.mark("sp")

    def squares(value):
        squared = value * value
        total = squared[0:8, 0:128]
        for a in range(BLK // 8):
            for b in range(LANES // 128):
                if a or b:
                    total = total + squared[a * 8:a * 8 + 8, b * 128:b * 128 + 128]
        return total

    sums = {}

    def norm(kind, it, axes):
        yield need(*[("sum", kind, it, h) for h in range(HALVES)])
        total = sums[kind, it, 0]
        for h in range(1, HALVES):
            total = total + sums[kind, it, h]
        flush(("n", kind))
        for axis in axes:
            buf = {"x": nx, "y": ny, "z": nz}[axis]
            size = SIZE[axis]
            nown[kind, "xyz".index(axis)] = total
            buf[kind, me[axis]] = total
            for d in sorted(range(1, size), key=lambda d: -min(d, size - d)):
                send(it, ("n", kind, axis), nown.at[kind, "xyz".index(axis)], buf.at[kind, me[axis]],
                     axis, d, ("n", kind))
            yield from wait_recv(it, ("n", kind, axis), (size - 1) * 4096)
            total = buf[kind, 0]
            for i in range(1, size):
                total = total + buf[kind, i]
            spend(0.05)
        sums[kind, it] = jnp.sqrt(jnp.sum(total, axis=(0, 1), keepdims=True) / COUNT)
        spend(0.2)
        plan.mark(("norm", kind, it))

    def gather_x(it, h):
        yield need(("left", it, h))
        flush(("gx", h))
        value = left[h]
        uall[h, x] = value
        for d in (2, 1, 3):
            send(it, ("gx", h), uall.at[h, x], uall.at[h, x], "x", d, ("gx", h))
        sums[0, it, h] = squares(value)
        spend(0.15)
        plan.mark(("sum", 0, it, h))
        yield from wait_recv(it, ("gx", h), 3 * size_of(uall.at[h, 0]))
        plan.mark(("gx", it, h))
        yield need("kt3")
        flush(("gr", h), ("sx", h))
        value = uall[h].reshape(ROWS_REC, LANES)
        real, imag = value[:, :WIDE], value[:, WIDE:]
        for base, both in ((0, (real, imag)), (ROWS_REC, (imag, -real))):
            for i in range(2):
                cols = slice(i * WIDE, i * WIDE + WIDE)
                high = both[i].astype(BF16)
                wst[base:base + ROWS_REC, cols] = high
                wst[base + 320:base + 320 + ROWS_REC, cols] = high
                wst[base + 640:base + 640 + ROWS_REC, cols] = (both[i] - high.astype(F32)).astype(BF16)

        def tile(i, carry):
            start = pl.multiple_of(i * 320, 320)
            out = jnp.dot(kt3[pl.ds(start, 320), :], wst[...], preferred_element_type=F32)
            p[h, pl.ds(i * 2, 2)] = out.reshape(2, NY, BLK, LANES)
            return carry

        lax.fori_loop(0, 4, tile, 0)
        spend(1.2)
        plan.mark(("p", it, h))

    ORDER = (4, 3, 5, 2, 6, 1, 7, 0)
    A, B = pl.ds(0, 16), pl.ds(16, 24)

    def za(it, h):
        yield need(("p", it, h))
        for way in WAYS:
            part = rows_a(way, True)
            send(it, ("za", h, way), p.at[h, at("z", 3 * way), :, A], rza1.at[h, ii(way), :, pl.ds(0, 16)],
                 "z", way, ("sr", h))
            send(it, ("za", h, way), p.at[h, at("z", 4 * way), :, part], rza1.at[h, ii(way), :, pl.ds(16, 8)],
                 "z", 2 * way, ("sr", h))
        for way in WAYS:
            send(it, ("za", h), p.at[h, at("z", way), :, A], rza2.at[h, ii(way)], "z", way, ("sr", h))
        for way in WAYS:
            yield from wait_recv(it, ("za", h, way), size_of(rza1.at[h, 0]))
            p[h, at("z", 2 * way), :, A] += rza1[h, ii(way), :, 0:16]
            p[h, at("z", 2 * way), :, rows_a(way, True)] += rza1[h, ii(way), :, 16:24]
            spend(0.12)
            send(it, ("za", h), p.at[h, at("z", 2 * way), :, A], rza2.at[h, 2 + ii(way)], "z", 2 * way, ("sr", h))
        yield from wait_recv(it, ("za", h), size_of(rza2.at[h]))
        p[h, z, :, A] += rza2[h, 0] + rza2[h, 1] + rza2[h, 2] + rza2[h, 3]
        spend(0.15)
        for d in (2, 1, 3):
            send(it, ("ya", h), p.at[h, z, at("y", d), A], rya.at[h, d - 1], "y", d, ("sr", h))
        yield from wait_recv(it, ("ya", h), size_of(rya.at[h]))
        p[h, z, y, A] += rya[h, 0] + rya[h, 1] + rya[h, 2]
        spend(0.06)
        plan.mark(("za", it, h))

    def yb(it, h, d):
        k = ORDER.index(d)
        if k < AHEAD:
            yield need(("p", it, h))
        else:
            yield need(("yb", it, h, ORDER[k - AHEAD]))
        for e in (2, 1, 3):
            send(it, ("yb", h, d), p.at[h, at("z", d), at("y", e), B], ryb.at[h, d, e - 1], "y", e, ("sr", h))
        yield from wait_recv(it, ("yb", h, d), size_of(ryb.at[h, 0]))
        p[h, at("z", d), y, B] += ryb[h, d, 0] + ryb[h, d, 1] + ryb[h, d, 2]
        spend(0.08)
        plan.mark(("yb", it, h, d))

    def zb(it, h, way):
        part = rows_b(way, True)
        yield need(("yb", it, h, 4))
        send(it, ("zb", h, way), p.at[h, at("z", 4 * way), y, part], rzb1.at[h, ii(way), pl.ds(24, part.size)],
             "z", 2 * way, ("sr", h))
        yield need(("yb", it, h, 3 * way % NZ))
        send(it, ("zb", h, way), p.at[h, at("z", 3 * way), y, B], rzb1.at[h, ii(way), pl.ds(0, 24)],
             "z", way, ("sr", h))
        yield need(("yb", it, h, 2 * way % NZ))
        yield from wait_recv(it, ("zb", h, way), (24 + part.size) * 4 * LANES)
        p[h, at("z", 2 * way), y, B] += rzb1[h, ii(way), 0:24]
        p[h, at("z", 2 * way), y, part] += rzb1[h, ii(way), 24:24 + part.size]
        spend(0.06)
        send(it, ("zb", h), p.at[h, at("z", 2 * way), y, B], rzb2.at[h, 2 + ii(way)], "z", 2 * way, ("sr", h))
        plan.mark(("zb", it, h, way))

    def zb_end(it, h):
        for way in WAYS:
            yield need(("yb", it, h, way % NZ))
            send(it, ("zb", h), p.at[h, at("z", way), y, B], rzb2.at[h, ii(way)], "z", way, ("sr", h))
        yield need(("yb", it, h, 0), *[("zb", it, h, way) for way in WAYS])
        yield from wait_recv(it, ("zb", h), size_of(rzb2.at[h]))
        p[h, z, y, B] += rzb2[h, 0] + rzb2[h, 1] + rzb2[h, 2] + rzb2[h, 3]
        spend(0.08)
        plan.mark(("zb", it, h))

    state = {}

    def right(it, h):
        yield need(("norm", 0, it), ("za", it, h), ("zb", it, h))
        beta = sums[0, it]
        value = p[h, z, y] / beta
        if it:
            value = value - beta * state["v", h]
        vall[h, z, y] = value
        state["right", h] = value
        spend(0.1)
        plan.mark(("right", it, h))
        sums[1, it, h] = squares(value)
        spend(0.15)
        plan.mark(("sum", 1, it, h))

    def bz(it, h):
        yield need(("right", it, h))
        own = vall.at[h, z, y, B]
        for d in (2, -2, 1, -1):
            send(it, ("bz", h, -d % NZ), own, own, "z", d, ("gr", h))
        for way in WAYS:
            yield from wait_recv(it, ("bz", h, -2 * way % NZ), 24 * 4 * LANES)
            block = vall.at[h, at("z", -2 * way), y, rows_b(way, True)]
            send(it, ("bz", h, 4), block, block, "z", 2 * way, ("gr", h))
            block = vall.at[h, at("z", -2 * way), y, B]
            send(it, ("bz", h, -3 * way % NZ), block, block, "z", way, ("gr", h))
            plan.mark(("bz", it, h, -2 * way % NZ))

    def by(it, h, d):
        if d == 0:
            yield need(("right", it, h))
        elif d in (2, 6):
            yield need(("bz", it, h, d))
        else:
            yield from wait_recv(it, ("bz", h, d), 24 * 4 * LANES)
        block = vall.at[h, at("z", d), y, B]
        for e in (2, 1, 3):
            send(it, ("by", h), block, block, "y", e, ("gr", h))
        plan.mark(("by", it, h, d))

    def az(it, h):
        yield need(("right", it, h))
        own = vall.at[h, z, y, A]
        for d in (2, 1, 3):
            send(it, ("ay", h), own, own, "y", d, ("gr", h))
        yield from wait_recv(it, ("ay", h), 3 * 16 * 4 * LANES)
        own = vall.at[h, z, :, A]
        for d in (2, -2):
            send(it, ("az", h, d), own, own, "z", d, ("gr", h))
        for d in (1, -1):
            send(it, ("az", h), own, own, "z", d, ("gr", h))
        for way in WAYS:
            yield from wait_recv(it, ("az", h, 2 * way), 64 * 4 * LANES)
            block = vall.at[h, at("z", -2 * way), :, A]
            send(it, ("az", h), block, block, "z", way, ("gr", h))
            block = vall.at[h, at("z", -2 * way), :, rows_a(way, True)]
            send(it, ("az", h), block, block, "z", 2 * way, ("gr", h))
        yield from wait_recv(it, ("az", h), 5 * 64 * 4 * LANES)
        plan.mark(("az", it, h))

    def forward(it, h):
        yield need("sp", ("az", it, h), *[("by", it, h, d) for d in range(NZ)])
        yield from wait_recv(it, ("by", h), NZ * 3 * 24 * 4 * LANES)
        flush(("gx", h), ("sr", h))

        def parts(i, carry):
            value = vall[h, i].reshape(NY * BLK, LANES)
            high = value.astype(BF16)
            rows = pl.ds(pl.multiple_of(i * 160, 160), 160)
            vh[rows, :] = high
            vl[rows, :] = (value - high.astype(F32)).astype(BF16)
            return carry

        lax.fori_loop(0, NZ, parts, 0)

        def tile(i, carry):
            rows = pl.ds(pl.multiple_of(i * 320, 320), 320)
            acc[rows, :] = jnp.dot(sp[rows, :], vh[...], preferred_element_type=F32)
            return carry

        lax.fori_loop(0, 2, tile, 0)
        both = acc[0:320, :] + acc[320:640, :] + jnp.dot(sp[0:320, :], vl[...], preferred_element_type=F32)
        real = both[:ROWS_REC, :WIDE] - both[ROWS_REC:, WIDE:]
        imag = both[:ROWS_REC, WIDE:] + both[ROWS_REC:, :WIDE]
        q[h, :, :, :WIDE] = real.reshape(NX, BLK, WIDE)
        q[h, :, :, WIDE:] = imag.reshape(NX, BLK, WIDE)
        spend(1.4)
        for d in (2, 1, 3):
            send(it, ("sx", h), q.at[h, at("x", d)], rxq.at[h, d - 1], "x", d, ("sx", h))
        yield from wait_recv(it, ("sx", h), size_of(rxq.at[h]))
        product = q[h, x] + rxq[h, 0] + rxq[h, 1] + rxq[h, 2]
        yield need(("norm", 1, it))
        alpha, beta = sums[1, it], sums[0, it]
        value = product / alpha - alpha * (left[h] / beta)
        left[h] = value
        spend(0.15)
        plan.mark(("left", it + 1, h))
        vnew = state["right", h] / alpha
        if it == 0:
            state["w", h] = vnew
            state["sol", h] = jnp.zeros((BLK, LANES), F32)
        else:
            rho, cosine, sine, phibar = rotation(it - 1)
            state["sol", h] = state["sol", h] + (cosine * phibar / rho) * state["w", h]
            state["w", h] = vnew - (sine * alpha / rho) * state["w", h]
        state["v", h] = vnew
        spend(0.3)
        plan.mark(("state", it, h))

    known = {}

    def rotation(it):
        if it not in known:
            beta = sums[0, it + 1]
            if it == 0:
                rhobar, phibar = sums[1, 0], sums[0, 0]
            else:
                rho, cosine, sine, phibar = rotation(it - 1)
                rhobar, phibar = -cosine * sums[1, it], sine * phibar
            rho = jnp.sqrt(rhobar * rhobar + beta * beta)
            known[it] = (rho, rhobar / rho, beta / rho, phibar)
        return known[it]

    def output(i, h, out):
        if i == 0:
            yield need(("left", ITERS, h))
            value = left[h]
            sums[0, ITERS, h] = squares(value)
            plan.mark(("sum", 0, ITERS, h))
        else:
            yield need(("norm", 0, ITERS), ("state", ITERS - 1, h))
            rho, cosine, sine, phibar = rotation(ITERS - 1)
            value = state["sol", h] + (cosine * phibar / rho) * state["w", h]
        ostage[i, h, 0, 0:ROWS] = value[:ROWS]
        ostage[i, h, 1, 0:ROWS] = value[ROWS:]
        spend(0.2)
        send(0, ("out", i, h), ostage.at[i, h, oc], orecv.at[i, h], "c", 0, "out")
        yield from wait_recv(0, ("out", i, h), size_of(orecv.at[i, h]))
        mine = ostage[i, h, c, 0:ROWS]
        other = orecv[i, h, 0:ROWS]
        slab = (jnp.where(c == 0, mine, other), jnp.where(c == 0, other, mine))
        for f in range(FREQS):
            for part in range(2):
                out[:, part, f, h * WIDE:h * WIDE + WIDE] = slab[f][:, part * WIDE:part * WIDE + WIDE]
        spend(0.2)

    plan.add(observe(), 0)
    for it in range(ITERS):
        plan.add(norm(0, it, "xyz"), 0)
        plan.add(norm(1, it, "yzx"), 0)
        for h in range(HALVES):
            plan.add(gather_x(it, h), 1 + h)
            plan.add(za(it, h), 1 + h)
            plan.add(zb_end(it, h), 1 + h)
            plan.add(bz(it, h), 1 + h)
            plan.add(az(it, h), 1 + h)
            for way in WAYS:
                plan.add(zb(it, h, way), 1 + h)
            for d in ORDER:
                plan.add(yb(it, h, d), 1 + h)
            for d in (0, 1, 7, 2, 6, 3, 5, 4):
                plan.add(by(it, h, d), 1 + h)
            plan.add(right(it, h), 1 + h)
            plan.add(forward(it, h), 1 + h)
    plan.add(norm(0, ITERS, "xyz"), 0)
    for h in range(HALVES):
        plan.add(output(0, h, left_out), 3)
        plan.add(output(1, h, sol_out), 2)
    plan.add(order_kernel(), 5)
    plan.run()
    flush(*list(pending))
    TOTAL.append((plan.now, dict(plan.events), (len(plan.numbers), len(groups))))


TOTAL = []


def on_device(kernel, traces, acq_lists, counts):
    vmem = pltpu.VMEM
    two = HALVES
    scratch = [
        vmem((2, 2, ROWS_REC, 640), F32),
        vmem((960, COLS), BF16),
        vmem((640, COLS), BF16),
        vmem((COLS, 960), BF16),
        vmem((COLS, COLS), BF16),
        vmem((two, NZ, NY, BLK, LANES), F32),
        vmem((two, NZ, NY, BLK, LANES), F32),
        vmem((COLS, LANES), BF16),
        vmem((COLS, LANES), BF16),
        vmem((960, LANES), BF16),
        vmem((two, NX, BLK, LANES), F32),
        vmem((two, NX, BLK, LANES), F32),
        vmem((640, LANES), F32),
        vmem((64, two * LANES), F32),
        vmem((32, two * LANES), F32),
        vmem((8, 128), jnp.int32),
        vmem((8, 128), jnp.int32),
        vmem((NZ, 8, two * LANES + 128), F32),
        vmem((64, two * LANES + 128), F32),
        vmem((NY, 16, two * LANES + 128), F32),
        vmem((NY, 16, two * LANES + 128), F32),
        vmem((two, 2, NY, 24, LANES), F32),
        vmem((two, 4, NY, 16, LANES), F32),
        vmem((two, NZ, 3, 24, LANES), F32),
        vmem((two, 2, 40, LANES), F32),
        vmem((two, 4, 24, LANES), F32),
        vmem((two, 3, 16, LANES), F32),
        vmem((two, 3, BLK, LANES), F32),
        vmem((8192, 128), F32),
        vmem((2, 3, 8, 128), F32),
        vmem((2, NX, 8, 128), F32),
        vmem((2, NY, 8, 128), F32),
        vmem((2, NZ, 8, 128), F32),
        vmem((two, BLK, LANES), F32),
        vmem((2, two, 2, 24, LANES), F32),
        vmem((2, two, 24, LANES), F32),
        pltpu.SemaphoreType.DMA((GROUPS,)),
        pltpu.SemaphoreType.DMA((COPIES,)),
        pltpu.SemaphoreType.DMA((1,)),
    ]
    whole = pl.BlockSpec(memory_space=pltpu.VMEM)
    return pl.pallas_call(
        kernel_body,
        out_shape=(jax.ShapeDtypeStruct((ROWS, 2, FREQS, SOURCES), F32),) * 2,
        in_specs=[pl.BlockSpec(memory_space=pl.ANY), whole, whole, whole],
        out_specs=(whole, whole),
        scratch_shapes=scratch,
        compiler_params=pltpu.CompilerParams(
            collective_id=0, has_side_effects=True, vmem_limit_bytes=60 * 1024 * 1024),
    )(kernel, traces, acq_lists, counts)


def solution(mesh):
    placed = (
        P(None, None, "rec", "src"),
        P("src", "rec", None, None, None),
        P("src", "rec"),
        P("src", "rec"),
    )
    return jax.shard_map(
        on_device,
        mesh=mesh,
        in_specs=placed,
        out_specs=(P(("src", "rec"), None, None, None), P(("rec", "src"), None, None, None)),
        check_vma=False,
    )
```

```python
import random
import jax
import jax.numpy as jnp
from jax import lax
from jax.experimental import pallas as pl
from jax.experimental.pallas import tpu as pltpu
from jax.sharding import PartitionSpec as P

NR = 5120
FREQS = 2
SOURCES = 256
ITERS = 2
NZ, NY, NX = 8, 4, 4
SIZE = {"x": NX, "y": NY, "z": NZ, "w": NX * NY}
ROWS = 20
HALVES = 2
WIDE = SOURCES // HALVES
LANES = 2 * WIDE
BLK = 40
ROWS_REC = 160
COLS = 1280
COPIES = 71
GROUPS = 16
AHEAD = 4
SEED = 0
NOISE = (0,)
ZA_RELAY = ()
AZ_RELAY = ()
YB_RELAY = ()
BY_RELAY = ()
MESH = pl.DeviceIdType.MESH
F32 = jnp.float32
BF16 = jnp.bfloat16
COUNT = 2.0 * NR * SOURCES
EXACT = lax.Precision.HIGHEST
NEVER = 1e9

RATE = 51e3
RATE_CHIP = 600e3
DELAY = {("c", 0): 0.9, ("z", 1): 2.5, ("z", 2): 3.1, ("z", 3): 3.7, ("z", 4): 4.3}
DELAY.update({(a, d): 2.8 + 0.2 * d for a in "xy" for d in (1, 2)})
WAYS = (1, -1)


class Plan:
    def __init__(self):
        self.now = 0.0
        self.noise = random.Random(SEED)
        self.link = {}
        self.arrived = {}
        self.counted = {}
        self.expected = {}
        self.events = {}
        self.numbers = {}
        self.tasks = []
        self.log = []

    def number(self, name):
        return self.numbers.setdefault(name, len(self.numbers))

    def add(self, task, rank=0):
        rank += self.noise.choice(NOISE)
        self.tasks.append([rank, len(self.log), task, None])
        self.log.append(rank)
        self.step(self.tasks[-1])

    def sent(self, key, axis, d, size):
        hops = min(d % SIZE[axis], -d % SIZE[axis]) if axis != "c" else 0
        if axis == "w":
            dx, dy = d % NX, d // NX
            far = min(dx, NX - dx) + min(dy, NY - dy)
            self.arrived[key] = max(self.arrived.get(key, 0.0), self.now + 2.3 + 0.6 * far)
            self.counted[key] = self.counted.get(key, 0) + size
            return
        if axis == "c":
            paths, load = [axis], size / RATE_CHIP
        elif 2 * hops == SIZE[axis]:
            paths, load = [(axis, 1), (axis, -1)], size * hops / 2 / RATE
        else:
            paths, load = [(axis, 1 if d % SIZE[axis] == hops else -1)], size * hops / RATE
        start = max([self.now] + [self.link.get(path, 0.0) for path in paths])
        for path in paths:
            self.link[path] = start + load
        came = start + load + DELAY[axis, hops]
        self.arrived[key] = max(self.arrived.get(key, 0.0), came)
        self.counted[key] = self.counted.get(key, 0) + size

    def mark(self, name):
        self.events[name] = self.now

    def ready(self, need):
        if need is None:
            return 0.0
        if need[0] == "r":
            if self.counted.get(need[1], 0) < need[2]:
                return NEVER
            return self.arrived[need[1]]
        return max(self.events.get(name, NEVER) for name in need[1])

    def step(self, entry):
        try:
            entry[3] = next(entry[2])
        except StopIteration:
            self.tasks.remove(entry)

    def run(self):
        while self.tasks:
            times = [self.ready(entry[3]) for entry in self.tasks]
            first = min(times)
            if first >= NEVER:
                raise ValueError("stuck")
            self.now = max(self.now, first)
            able = [e for e, t in zip(self.tasks, times) if t <= self.now]
            best = min(able, key=lambda e: (e[0], self.ready(e[3]), e[1]))
            self.step(best)


def rows_a(way, part):
    return pl.ds(0 if way == 1 else 8, 8) if part else pl.ds(0, 16)


def rows_b(way, part):
    if not part:
        return pl.ds(16, 24)
    return pl.ds(16, 16) if way == 1 else pl.ds(32, 8)


def ii(way):
    return 0 if way == 1 else 1


def kernel_body(k_hbm, traces_hbm, ids_ref, counts_ref, sol_out, left_out, *scratch):
    (traces, kf, s3, sp, kt3, pick, p, vall, vh, vl, wst, uall, q, acc, tbuf, tsend, meta, mbuf,
     send_e, recv_e1, send_e2, recv_e2, rza1, rza2, ryb, rzb1, rzb2, rya, rxq, dummy, tiny, nown, nx, nz,
     left, ostage, orecv, ssem, rsem, lsem) = scratch
    plan = Plan()
    r = lax.axis_index("rec")
    s = lax.axis_index("src")
    z, y = r // NY, r % NY
    x, c = s // 2, s % 2
    oc = 1 - c
    me = {"x": x, "y": y, "z": z}

    def at(axis, d):
        return lax.rem(me[axis] + d + 2 * SIZE[axis], SIZE[axis])

    def dev(axis, d):
        zz = at("z", d) if axis == "z" else z
        yy = at("y", d // NX if axis == "w" else d) if axis in "yw" else y
        xx = at("x", d % NX if axis == "w" else d) if axis in "xw" else x
        return (zz * NY + yy, xx * 2 + (oc if axis == "c" else c))

    pending = {}
    groups = {}

    def size_of(ref):
        size = 4
        for n in ref.shape:
            size *= n
        return size

    def waiting(size, i, sems):
        rows = (dummy if size % 4096 == 0 else tiny).at[pl.ds(0, size // 512)]
        return pltpu.make_async_copy(rows, rows, sems.at[i])

    def send(it, name, src, dst, axis, d, group):
        i = plan.number(name)
        g = groups.setdefault(group, len(groups))
        pltpu.make_async_remote_copy(
            src_ref=src, dst_ref=dst, send_sem=ssem.at[g], recv_sem=rsem.at[i],
            device_id=dev(axis, d), device_id_type=MESH).start()
        pending[group] = pending.get(group, 0) + size_of(src)
        plan.sent((it, name), axis, d, size_of(src))

    def wait_recv(it, name, size):
        yield ("r", (it, name), size)
        waiting(size, plan.number(name), rsem).wait()

    def flush(*names):
        for group in names:
            size = pending.pop(group, 0)
            if size:
                waiting(size, groups[group], ssem).wait()

    def need(*names):
        return ("e", names)

    def spend(us):
        plan.now += us

    own_k = pltpu.make_async_copy(k_hbm.at[:, c], kf.at[:, c], lsem.at[0])
    own_k.start()
    own_t = pltpu.make_async_copy(traces_hbm, traces, lsem.at[1])
    own_t.start()
    barrier = pltpu.get_barrier_semaphore()
    friends = [(a, d) for a in ("z", "w") for d in range(1, SIZE[a])] + [("c", 0)]
    for friend in friends:
        pl.semaphore_signal(barrier, inc=1, device_id=dev(*friend), device_id_type=MESH)

    slots = traces_hbm.shape[1]
    lane_row = lax.broadcasted_iota(jnp.int32, (1, slots), 1)
    listed = jnp.where(lane_row < counts_ref[...], ids_ref[...], -1)
    meta[...] = jnp.full((8, 128), -1, jnp.int32)

    @pl.when(c == 0)
    def _():
        meta[0:1, 0:slots] = listed

    @pl.when(c == 1)
    def _():
        meta[0:1, 32:32 + slots] = listed

    blank = jnp.zeros((32, HALVES * LANES), F32)
    tbuf[pl.ds(pl.multiple_of(c * 32, 32), 32), :] = blank
    tsend[...] = blank
    own_t.wait()
    for half in range(HALVES):
        for part in range(2):
            cols = slice(half * LANES + part * WIDE, half * LANES + part * WIDE + WIDE)
            lanes = slice(half * WIDE, half * WIDE + WIDE)
            slab0 = traces[0, :, part, 0, lanes]
            slab1 = traces[0, :, part, 1, lanes]
            tsend[0:slots, cols] = jnp.where(c == 0, slab1, slab0)
            tbuf[pl.ds(pl.multiple_of(c * 32, 32), slots), cols] = jnp.where(c == 0, slab0, slab1)
    pl.semaphore_wait(barrier, len(friends))
    send(0, "meta", meta, mbuf, "c", 0, "in")
    send(0, "traces", tsend, tbuf.at[pl.ds(c * 32, 32)], "c", 0, "in")
    send(0, "k", k_hbm.at[:, oc], kf.at[:, c], "c", 0, "in")

    row = lax.broadcasted_iota(jnp.int32, (64, 128), 0)
    lane = lax.broadcasted_iota(jnp.int32, (64, 128), 1)
    wide = HALVES * LANES

    def observe():
        yield from wait_recv(0, "meta", 4096)
        yield from wait_recv(0, "traces", size_of(tsend))
        ids = jnp.maximum(meta[0:1, :], mbuf[0:1, :])
        area = (row >> 3) * NY + (row & 3)
        offset = ids - ROWS * area
        match = (offset >= 0) & (offset < ROWS) & ((lane >> 5) == ((row >> 2) & 1))
        picked = jnp.dot(jnp.where(match, 1.0, 0.0)[:, :64], tbuf[...],
                         preferred_element_type=F32, precision=EXACT)
        place = jnp.sum(jnp.where(match, (offset + 1).astype(F32), 0.0), axis=1, keepdims=True)
        send_e[:, :, 0:wide] = picked.reshape(NZ, 8, wide)
        send_e[:, :, wide:] = jnp.broadcast_to(place, (64, 128)).reshape(NZ, 8, 128)
        spend(0.8)
        mine = pl.ds(pl.multiple_of(z * 8, 8), 8)
        for d in (4, 3, 5, 2, 6, 1, 7):
            send(0, "e1", send_e.at[at("z", d)], recv_e1.at[mine], "z", d, "in")
        recv_e1[mine, :] = send_e[z]
        yield from wait_recv(0, "e1", 7 * size_of(send_e.at[0]))
        swap = jnp.where(lane == (row & 15) * 4 + (row >> 4), 1.0, 0.0)[:, :64]
        send_e2[...] = jnp.dot(swap, recv_e1[...], preferred_element_type=F32,
                               precision=EXACT).reshape(NY, 16, wide + 128)
        spend(0.8)
        for d in (2, 1, 3):
            send(0, "e2", send_e2.at[at("y", d)], recv_e2.at[y], "y", d, "in")
        recv_e2[y] = send_e2[y]
        yield from wait_recv(0, "e2", 3 * size_of(send_e2.at[0]))
        got = recv_e2[...].reshape(64, wide + 128)
        slot = got[:, wide:]
        wanted = slot - 1.0 + jnp.where((row & 1) == 1, float(ROWS), 0.0)
        onehot = jnp.where((slot > 0.5) & (lane.astype(F32) == wanted), 1.0, 0.0)
        value = jnp.dot(jnp.transpose(onehot)[:BLK, :], got[:, :wide],
                        preferred_element_type=F32, precision=EXACT)
        spend(0.8)
        for h in range(HALVES):
            left[h] = value[:, h * LANES:h * LANES + LANES]
            plan.mark(("left", 0, h))

    def split_half(half):
        for part in range(2):
            cols = pl.ds(pl.multiple_of(half * 640, 128), 640)
            value = kf[part, half]
            high = value.astype(BF16)
            low = (value - high.astype(F32)).astype(BF16)
            base = part * ROWS_REC
            s3[base:base + ROWS_REC, cols] = high
            s3[base + 320:base + 320 + ROWS_REC, cols] = low
            s3[base + 640:base + 640 + ROWS_REC, cols] = high

    dims = (((1,), (1,)), ((), ()))

    def order_kernel():
        def build(i, carry):
            start = pl.multiple_of(i * 256, 256)
            new = lax.broadcasted_iota(jnp.int32, (256, 128), 0) + start
            rec = (new * 1639) >> 16
            rest = new - rec * BLK
            old = jnp.where(rest >= ROWS, 640 - ROWS, 0) + rec * ROWS + rest
            lanes = lax.broadcasted_iota(jnp.int32, (256, 128), 1)
            for j in range(COLS // 128):
                pick[pl.ds(start, 256), j * 128:j * 128 + 128] = jnp.where(
                    lanes + j * 128 == old, 1.0, 0.0).astype(BF16)
            return carry

        lax.fori_loop(0, COLS // 256, build, 0)
        spend(1.5)
        own_k.wait()
        split_half(c)
        spend(0.4)
        yield from wait_recv(0, "k", size_of(kf.at[:, 0]))
        split_half(oc)
        spend(0.4)

        def turned(i, carry):
            start = pl.multiple_of(i * 256, 256)
            kt3[pl.ds(start, 256), :] = lax.dot_general(
                pick[pl.ds(start, 256), :], s3[...], dims, preferred_element_type=F32).astype(BF16)
            return carry

        lax.fori_loop(0, COLS // 256, turned, 0)
        spend(3.0)
        plan.mark("kt3")
        yield need(("left", 0, 0))

        def straight(i, carry):
            start = pl.multiple_of(i * 256, 256)
            sp[:, pl.ds(start, 256)] = lax.dot_general(
                s3[0:640, :], pick[pl.ds(start, 256), :], dims, preferred_element_type=F32).astype(BF16)
            return carry

        yield need(("gx", 0, HALVES - 1))
        lax.fori_loop(0, COLS // 256, straight, 0)
        spend(2.5)
        plan.mark("sp")

    def squares(value):
        squared = value * value
        total = squared[0:8, 0:128]
        for a in range(BLK // 8):
            for b in range(LANES // 128):
                if a or b:
                    total = total + squared[a * 8:a * 8 + 8, b * 128:b * 128 + 128]
        return total

    sums = {}

    def norm(kind, it, axes):
        yield need(*[("sum", kind, it, h) for h in range(HALVES)])
        total = sums[kind, it, 0]
        for h in range(1, HALVES):
            total = total + sums[kind, it, h]
        total = jnp.sum(total, axis=0, keepdims=True)
        flush(("n", kind))
        for axis in axes:
            buf = {"w": nx, "z": nz}[axis]
            size = SIZE[axis]
            mine = z if axis == "z" else y * NX + x
            nown[kind, "wz".index(axis)] = total
            buf[kind, mine] = total
            for d in range(1, size):
                send(it, ("n", kind, axis), nown.at[kind, "wz".index(axis)], buf.at[kind, mine],
                     axis, d, ("n", kind))
            yield from wait_recv(it, ("n", kind, axis), (size - 1) * 512)
            total = buf[kind, 0]
            for i in range(1, size):
                total = total + buf[kind, i]
            spend(0.1)
        sums[kind, it] = jnp.sqrt(jnp.sum(total, axis=(0, 1), keepdims=True) / COUNT)
        spend(0.2)
        plan.mark(("norm", kind, it))

    def gather_x(it, h):
        yield need(("left", it, h))
        flush(("gx", h))
        value = left[h]
        uall[h, x] = value
        for d in (2, 1, 3):
            send(it, ("gx", h), uall.at[h, x], uall.at[h, x], "x", d, ("gx", h))
        sums[0, it, h] = squares(value)
        spend(0.15)
        plan.mark(("sum", 0, it, h))
        yield from wait_recv(it, ("gx", h), 3 * size_of(uall.at[h, 0]))
        plan.mark(("gx", it, h))
        yield need("kt3")
        flush(("gr", h), ("sx", h))
        value = uall[h].reshape(ROWS_REC, LANES)
        real, imag = value[:, :WIDE], value[:, WIDE:]
        for base, both in ((0, (real, imag)), (ROWS_REC, (imag, -real))):
            for i in range(2):
                cols = slice(i * WIDE, i * WIDE + WIDE)
                high = both[i].astype(BF16)
                wst[base:base + ROWS_REC, cols] = high
                wst[base + 320:base + 320 + ROWS_REC, cols] = high
                wst[base + 640:base + 640 + ROWS_REC, cols] = (both[i] - high.astype(F32)).astype(BF16)

        def tile(i, carry):
            start = pl.multiple_of(i * 320, 320)
            out = jnp.dot(kt3[pl.ds(start, 320), :], wst[...], preferred_element_type=F32)
            p[h, pl.ds(i * 2, 2)] = out.reshape(2, NY, BLK, LANES)
            return carry

        lax.fori_loop(0, 4, tile, 0)
        spend(1.2)
        plan.mark(("p", it, h))

    ORDER = (4, 3, 5, 2, 6, 1, 7, 0)
    A, B = pl.ds(0, 16), pl.ds(16, 24)

    def za(it, h):
        yield need(("p", it, h))
        if h in ZA_RELAY:
            yield need(*[("zr", it, h, g) for g in range(2)])
        else:
            for way in WAYS:
                part = rows_a(way, True)
                send(it, ("za", h, way), p.at[h, at("z", 3 * way), :, A], rza1.at[h, ii(way), :, pl.ds(0, 16)],
                     "z", way, ("sr", h))
                send(it, ("za", h, way), p.at[h, at("z", 4 * way), :, part], rza1.at[h, ii(way), :, pl.ds(16, 8)],
                     "z", 2 * way, ("sr", h))
            for way in WAYS:
                send(it, ("za", h), p.at[h, at("z", way), :, A], rza2.at[h, ii(way)], "z", way, ("sr", h))
            for way in WAYS:
                yield from wait_recv(it, ("za", h, way), size_of(rza1.at[h, 0]))
                p[h, at("z", 2 * way), :, A] += rza1[h, ii(way), :, 0:16]
                p[h, at("z", 2 * way), :, rows_a(way, True)] += rza1[h, ii(way), :, 16:24]
                spend(0.12)
                send(it, ("za", h), p.at[h, at("z", 2 * way), :, A], rza2.at[h, 2 + ii(way)], "z", 2 * way, ("sr", h))
            yield from wait_recv(it, ("za", h), size_of(rza2.at[h]))
            p[h, z, :, A] += rza2[h, 0] + rza2[h, 1] + rza2[h, 2] + rza2[h, 3]
        spend(0.15)
        for d in (2, 1, 3):
            send(it, ("ya", h), p.at[h, z, at("y", d), A], rya.at[h, d - 1], "y", d, ("sr", h))
        yield from wait_recv(it, ("ya", h), size_of(rya.at[h]))
        p[h, z, y, A] += rya[h, 0] + rya[h, 1] + rya[h, 2]
        spend(0.06)
        plan.mark(("za", it, h))

    def zr(it, h, g):
        yield need(("p", it, h))
        pair = pl.ds(2 * g, 2)
        for way in WAYS:
            part = rows_a(way, True)
            send(it, ("zr", h, g, way, 1), p.at[h, at("z", 4 * way), pair, part],
                 rza1.at[h, ii(way), pair, pl.ds(16, 8)], "z", way, ("sr", h))
        for step in (1, 2, 3):
            for way in WAYS:
                part = rows_a(way, True)
                yield from wait_recv(it, ("zr", h, g, way, step), (16 if step == 1 else 32) * 4 * LANES)
                d = at("z", (4 - step) * way)
                if step == 1:
                    p[h, d, pair, part] += rza1[h, ii(way), pair, 16:24]
                elif step == 2:
                    p[h, d, pair, A] += rza1[h, ii(way), pair, 0:16]
                else:
                    p[h, d, pair, A] += rza2[h, 2 + ii(way), pair]
                spend(0.06)
                into = (None, rza1.at[h, ii(way), pair, pl.ds(0, 16)], rza2.at[h, 2 + ii(way), pair],
                        rza2.at[h, ii(way), pair])[step]
                name = ("zr", h, g, way, step + 1) if step < 3 else ("zr", h, g)
                send(it, name, p.at[h, d, pair, A], into, "z", way, ("sr", h))
        yield from wait_recv(it, ("zr", h, g), 2 * 32 * 4 * LANES)
        p[h, z, pair, A] += rza2[h, 0, pair] + rza2[h, 1, pair]
        spend(0.08)
        plan.mark(("zr", it, h, g))

    def yb(it, h, d):
        k = ORDER.index(d)
        if k < AHEAD:
            yield need(("p", it, h))
        else:
            yield need(("yb", it, h, ORDER[k - AHEAD]))
        if d in YB_RELAY:
            for way in WAYS:
                part = rows_b(way if d % 2 else -way, True)
                send(it, ("yb", h, d, way), p.at[h, at("z", d), at("y", 2), part],
                     ryb.at[h, d, 2, pl.ds(part.start - 16, part.size)], "y", way, ("sr", h))
            for way in WAYS:
                part = rows_b(way if d % 2 else -way, True)
                yield from wait_recv(it, ("yb", h, d, way), part.size * 4 * LANES)
                p[h, at("z", d), at("y", way), part] += ryb[h, d, 2, part.start - 16:part.start - 16 + part.size]
                spend(0.05)
                send(it, ("yb", h, d), p.at[h, at("z", d), at("y", way), B], ryb.at[h, d, ii(way)], "y", way, ("sr", h))
            yield from wait_recv(it, ("yb", h, d), 2 * 24 * 4 * LANES)
            p[h, at("z", d), y, B] += ryb[h, d, 0] + ryb[h, d, 1]
        else:
            for e in (2, 1, 3):
                send(it, ("yb", h, d), p.at[h, at("z", d), at("y", e), B], ryb.at[h, d, e - 1], "y", e, ("sr", h))
            yield from wait_recv(it, ("yb", h, d), size_of(ryb.at[h, 0]))
            p[h, at("z", d), y, B] += ryb[h, d, 0] + ryb[h, d, 1] + ryb[h, d, 2]
        spend(0.08)
        plan.mark(("yb", it, h, d))

    def zb(it, h, way):
        part = rows_b(way, True)
        yield need(("yb", it, h, 4))
        send(it, ("zb", h, way), p.at[h, at("z", 4 * way), y, part], rzb1.at[h, ii(way), pl.ds(24, part.size)],
             "z", 2 * way, ("sr", h))
        yield need(("yb", it, h, 3 * way % NZ))
        send(it, ("zb", h, way), p.at[h, at("z", 3 * way), y, B], rzb1.at[h, ii(way), pl.ds(0, 24)],
             "z", way, ("sr", h))
        yield need(("yb", it, h, 2 * way % NZ))
        yield from wait_recv(it, ("zb", h, way), (24 + part.size) * 4 * LANES)
        p[h, at("z", 2 * way), y, B] += rzb1[h, ii(way), 0:24]
        p[h, at("z", 2 * way), y, part] += rzb1[h, ii(way), 24:24 + part.size]
        spend(0.06)
        send(it, ("zb", h), p.at[h, at("z", 2 * way), y, B], rzb2.at[h, 2 + ii(way)], "z", 2 * way, ("sr", h))
        plan.mark(("zb", it, h, way))

    def zb_end(it, h):
        for way in WAYS:
            yield need(("yb", it, h, way % NZ))
            send(it, ("zb", h), p.at[h, at("z", way), y, B], rzb2.at[h, ii(way)], "z", way, ("sr", h))
        yield need(("yb", it, h, 0), *[("zb", it, h, way) for way in WAYS])
        yield from wait_recv(it, ("zb", h), size_of(rzb2.at[h]))
        p[h, z, y, B] += rzb2[h, 0] + rzb2[h, 1] + rzb2[h, 2] + rzb2[h, 3]
        spend(0.08)
        plan.mark(("zb", it, h))

    state = {}

    def right(it, h):
        yield need(("norm", 0, it), ("za", it, h), ("zb", it, h))
        beta = sums[0, it]
        value = p[h, z, y] / beta
        if it:
            value = value - beta * state["v", h]
        vall[h, z, y] = value
        state["right", h] = value
        spend(0.1)
        plan.mark(("right", it, h))
        sums[1, it, h] = squares(value)
        spend(0.15)
        plan.mark(("sum", 1, it, h))

    def bz(it, h):
        yield need(("right", it, h))
        own = vall.at[h, z, y, B]
        for d in (2, -2, 1, -1):
            send(it, ("bz", h, -d % NZ), own, own, "z", d, ("gr", h))
        for way in WAYS:
            yield from wait_recv(it, ("bz", h, -2 * way % NZ), 24 * 4 * LANES)
            block = vall.at[h, at("z", -2 * way), y, rows_b(way, True)]
            send(it, ("bz", h, 4), block, block, "z", 2 * way, ("gr", h))
            block = vall.at[h, at("z", -2 * way), y, B]
            send(it, ("bz", h, -3 * way % NZ), block, block, "z", way, ("gr", h))
            plan.mark(("bz", it, h, -2 * way % NZ))

    def by(it, h, d):
        if d == 0:
            yield need(("right", it, h))
        elif d in (2, 6):
            yield need(("bz", it, h, d))
        else:
            yield from wait_recv(it, ("bz", h, d), 24 * 4 * LANES)
        block = vall.at[h, at("z", d), y, B]
        if d in BY_RELAY:
            for way in WAYS:
                send(it, ("by", h, d, way), block, block, "y", way, ("gr", h))
            plan.mark(("by", it, h, d))
            for way in WAYS:
                yield from wait_recv(it, ("by", h, d, way), 24 * 4 * LANES)
                block = vall.at[h, at("z", d), at("y", -way), rows_b(way if d % 2 else -way, True)]
                send(it, ("by", h), block, block, "y", way, ("gr", h))
        else:
            for e in (2, 1, 3):
                send(it, ("by", h), block, block, "y", e, ("gr", h))
        plan.mark(("by", it, h, d))

    def ar(it, h, g):
        yield need(("ay", it, h))
        pair = pl.ds(2 * g, 2)
        own = vall.at[h, z, pair, A]
        for way in WAYS:
            send(it, ("ar", h, g, way, 1), own, own, "z", way, ("gr", h))
        for step in (1, 2, 3):
            for way in WAYS:
                yield from wait_recv(it, ("ar", h, g, way, step), 32 * 4 * LANES)
                rows = A if step < 3 else rows_a(way, True)
                block = vall.at[h, at("z", -way * step), pair, rows]
                send(it, ("ar", h, g, way, step + 1) if step < 3 else ("ar", h, g), block, block, "z", way, ("gr", h))
        yield from wait_recv(it, ("ar", h, g), 32 * 4 * LANES)
        plan.mark(("ar", it, h, g))

    def az(it, h):
        yield need(("right", it, h))
        own = vall.at[h, z, y, A]
        for d in (2, 1, 3):
            send(it, ("ay", h), own, own, "y", d, ("gr", h))
        yield from wait_recv(it, ("ay", h), 3 * 16 * 4 * LANES)
        plan.mark(("ay", it, h))
        if h in AZ_RELAY:
            yield need(*[("ar", it, h, g) for g in range(2)])
            plan.mark(("az", it, h))
            return
        own = vall.at[h, z, :, A]
        for d in (2, -2):
            send(it, ("az", h, d), own, own, "z", d, ("gr", h))
        for d in (1, -1):
            send(it, ("az", h), own, own, "z", d, ("gr", h))
        for way in WAYS:
            yield from wait_recv(it, ("az", h, 2 * way), 64 * 4 * LANES)
            block = vall.at[h, at("z", -2 * way), :, A]
            send(it, ("az", h), block, block, "z", way, ("gr", h))
            block = vall.at[h, at("z", -2 * way), :, rows_a(way, True)]
            send(it, ("az", h), block, block, "z", 2 * way, ("gr", h))
        yield from wait_recv(it, ("az", h), 5 * 64 * 4 * LANES)
        plan.mark(("az", it, h))

    def forward(it, h):
        yield need("sp", ("az", it, h), *[("by", it, h, d) for d in range(NZ)])
        yield from wait_recv(it, ("by", h), (NZ * 3 - 2 * len(BY_RELAY)) * 24 * 4 * LANES)
        flush(("gx", h), ("sr", h))

        def parts(i, carry):
            value = vall[h, i].reshape(NY * BLK, LANES)
            high = value.astype(BF16)
            rows = pl.ds(pl.multiple_of(i * 160, 160), 160)
            vh[rows, :] = high
            vl[rows, :] = (value - high.astype(F32)).astype(BF16)
            return carry

        lax.fori_loop(0, NZ, parts, 0)

        def tile(i, carry):
            rows = pl.ds(pl.multiple_of(i * 320, 320), 320)
            acc[rows, :] = jnp.dot(sp[rows, :], vh[...], preferred_element_type=F32)
            return carry

        lax.fori_loop(0, 2, tile, 0)
        both = acc[0:320, :] + acc[320:640, :] + jnp.dot(sp[0:320, :], vl[...], preferred_element_type=F32)
        real = both[:ROWS_REC, :WIDE] - both[ROWS_REC:, WIDE:]
        imag = both[:ROWS_REC, WIDE:] + both[ROWS_REC:, :WIDE]
        q[h, :, :, :WIDE] = real.reshape(NX, BLK, WIDE)
        q[h, :, :, WIDE:] = imag.reshape(NX, BLK, WIDE)
        spend(1.4)
        for d in (2, 1, 3):
            send(it, ("sx", h), q.at[h, at("x", d)], rxq.at[h, d - 1], "x", d, ("sx", h))
        yield from wait_recv(it, ("sx", h), size_of(rxq.at[h]))
        product = q[h, x] + rxq[h, 0] + rxq[h, 1] + rxq[h, 2]
        yield need(("norm", 1, it))
        alpha, beta = sums[1, it], sums[0, it]
        value = product / alpha - alpha * (left[h] / beta)
        left[h] = value
        spend(0.15)
        plan.mark(("left", it + 1, h))
        vnew = state["right", h] / alpha
        if it == 0:
            state["w", h] = vnew
            state["sol", h] = jnp.zeros((BLK, LANES), F32)
        else:
            rho, cosine, sine, phibar = rotation(it - 1)
            state["sol", h] = state["sol", h] + (cosine * phibar / rho) * state["w", h]
            state["w", h] = vnew - (sine * alpha / rho) * state["w", h]
        state["v", h] = vnew
        spend(0.3)
        plan.mark(("state", it, h))

    known = {}

    def rotation(it):
        if it not in known:
            beta = sums[0, it + 1]
            if it == 0:
                rhobar, phibar = sums[1, 0], sums[0, 0]
            else:
                rho, cosine, sine, phibar = rotation(it - 1)
                rhobar, phibar = -cosine * sums[1, it], sine * phibar
            rho = jnp.sqrt(rhobar * rhobar + beta * beta)
            known[it] = (rho, rhobar / rho, beta / rho, phibar)
        return known[it]

    def output(i, h, out):
        if i == 0:
            yield need(("left", ITERS, h))
            value = left[h]
            sums[0, ITERS, h] = squares(value)
            plan.mark(("sum", 0, ITERS, h))
        else:
            yield need(("norm", 0, ITERS), ("state", ITERS - 1, h))
            rho, cosine, sine, phibar = rotation(ITERS - 1)
            value = state["sol", h] + (cosine * phibar / rho) * state["w", h]
        ostage[i, h, 0, 0:ROWS] = value[:ROWS]
        ostage[i, h, 1, 0:ROWS] = value[ROWS:]
        spend(0.2)
        send(0, ("out", i, h), ostage.at[i, h, oc], orecv.at[i, h], "c", 0, "out")
        yield from wait_recv(0, ("out", i, h), size_of(orecv.at[i, h]))
        mine = ostage[i, h, c, 0:ROWS]
        other = orecv[i, h, 0:ROWS]
        slab = (jnp.where(c == 0, mine, other), jnp.where(c == 0, other, mine))
        for f in range(FREQS):
            for part in range(2):
                out[:, part, f, h * WIDE:h * WIDE + WIDE] = slab[f][:, part * WIDE:part * WIDE + WIDE]
        spend(0.2)

    plan.add(observe(), 0)
    for it in range(ITERS):
        plan.add(norm(0, it, "wz"), 0)
        plan.add(norm(1, it, "zw"), 0)
        for h in range(HALVES):
            plan.add(gather_x(it, h), 1 + h)
            plan.add(za(it, h), 1 + h)
            plan.add(zb_end(it, h), 1 + h)
            plan.add(bz(it, h), 1 + h)
            plan.add(az(it, h), 1 + h)
            for g in range(2):
                if h in ZA_RELAY:
                    plan.add(zr(it, h, g), 1 + h)
                if h in AZ_RELAY:
                    plan.add(ar(it, h, g), 1 + h)
            for way in WAYS:
                plan.add(zb(it, h, way), 1 + h)
            for d in ORDER:
                plan.add(yb(it, h, d), 1 + h)
            for d in (0, 1, 7, 2, 6, 3, 5, 4):
                plan.add(by(it, h, d), 1 + h)
            plan.add(right(it, h), 1 + h)
            plan.add(forward(it, h), 1 + h)
    plan.add(norm(0, ITERS, "wz"), 0)
    for h in range(HALVES):
        plan.add(output(0, h, left_out), 3)
        plan.add(output(1, h, sol_out), 2)
    plan.add(order_kernel(), 5)
    plan.run()
    flush(*list(pending))
    TOTAL.append((plan.now, dict(plan.events), (len(plan.numbers), len(groups))))


TOTAL = []


def hand_over(sol_in, left_in, sol_out, left_out):
    sol_out[...] = sol_in[...]
    left_out[...] = left_in[...]


def on_device(kernel, traces, acq_lists, counts):
    vmem = pltpu.VMEM
    two = HALVES
    scratch = [
        vmem(traces.shape, F32),
        vmem((2, 2, ROWS_REC, 640), F32),
        vmem((960, COLS), BF16),
        vmem((640, COLS), BF16),
        vmem((COLS, 960), BF16),
        vmem((COLS, COLS), BF16),
        vmem((two, NZ, NY, BLK, LANES), F32),
        vmem((two, NZ, NY, BLK, LANES), F32),
        vmem((COLS, LANES), BF16),
        vmem((COLS, LANES), BF16),
        vmem((960, LANES), BF16),
        vmem((two, NX, BLK, LANES), F32),
        vmem((two, NX, BLK, LANES), F32),
        vmem((640, LANES), F32),
        vmem((64, two * LANES), F32),
        vmem((32, two * LANES), F32),
        vmem((8, 128), jnp.int32),
        vmem((8, 128), jnp.int32),
        vmem((NZ, 8, two * LANES + 128), F32),
        vmem((64, two * LANES + 128), F32),
        vmem((NY, 16, two * LANES + 128), F32),
        vmem((NY, 16, two * LANES + 128), F32),
        vmem((two, 2, NY, 24, LANES), F32),
        vmem((two, 4, NY, 16, LANES), F32),
        vmem((two, NZ, 3, 24, LANES), F32),
        vmem((two, 2, 40, LANES), F32),
        vmem((two, 4, 24, LANES), F32),
        vmem((two, 3, 16, LANES), F32),
        vmem((two, 3, BLK, LANES), F32),
        vmem((8192, 128), F32),
        vmem((64, 1, 128), F32),
        vmem((2, 2, 1, 128), F32),
        vmem((2, NX * NY, 1, 128), F32),
        vmem((2, NZ, 1, 128), F32),
        vmem((two, BLK, LANES), F32),
        vmem((2, two, 2, 24, LANES), F32),
        vmem((2, two, 24, LANES), F32),
        pltpu.SemaphoreType.DMA((GROUPS,)),
        pltpu.SemaphoreType.DMA((COPIES,)),
        pltpu.SemaphoreType.DMA((2,)),
    ]
    whole = pl.BlockSpec(memory_space=pltpu.VMEM)
    made = pl.pallas_call(
        kernel_body,
        out_shape=(jax.ShapeDtypeStruct((ROWS, 2, FREQS, SOURCES), F32),) * 2,
        in_specs=[pl.BlockSpec(memory_space=pl.ANY)] * 2 + [whole, whole],
        out_specs=(whole, whole),
        scratch_shapes=scratch,
        compiler_params=pltpu.CompilerParams(
            collective_id=0, has_side_effects=True, vmem_limit_bytes=60 * 1024 * 1024),
    )(kernel, traces, acq_lists, counts)
    return pl.pallas_call(
        hand_over,
        out_shape=(jax.ShapeDtypeStruct((ROWS, 2, FREQS, SOURCES), F32),) * 2,
        in_specs=[whole, whole],
        out_specs=(whole, whole),
    )(*made)


def solution(mesh):
    placed = (
        P(None, None, "rec", "src"),
        P("src", "rec", None, None, None),
        P("src", "rec"),
        P("src", "rec"),
    )
    return jax.shard_map(
        on_device,
        mesh=mesh,
        in_specs=placed,
        out_specs=(P(("src", "rec"), None, None, None), P(("rec", "src"), None, None, None)),
        check_vma=False,
    )
```

```python
import random
import jax
import jax.numpy as jnp
from jax import lax
from jax.experimental import pallas as pl
from jax.experimental.pallas import tpu as pltpu
from jax.sharding import PartitionSpec as P

NR = 5120
FREQS = 2
SOURCES = 256
ITERS = 2
NZ, NY, NX = 8, 4, 4
SIZE = {"x": NX, "y": NY, "z": NZ, "w": NX * NY}
ROWS = 20
HALVES = 2
WIDE = SOURCES // HALVES
LANES = 2 * WIDE
BLK = 40
ROWS_REC = 160
COLS = 1280
COPIES = 71
GROUPS = 16
AHEAD = 4
SEED = 0
NOISE = (0,)
ZA_RELAY = ()
AZ_RELAY = ()
YB_RELAY = ()
BY_RELAY = ()
MESH = pl.DeviceIdType.MESH
F32 = jnp.float32
BF16 = jnp.bfloat16
COUNT = 2.0 * NR * SOURCES
EXACT = lax.Precision.HIGHEST
NEVER = 1e9

RATE = 51e3
RATE_CHIP = 600e3
DELAY = {("c", 0): 0.9, ("z", 1): 1.9, ("z", 2): 2.5, ("z", 3): 3.1, ("z", 4): 3.7}
DELAY.update({(a, d): 2.2 + 0.2 * d for a in "xy" for d in (1, 2)})
WAYS = (1, -1)


class Plan:
    def __init__(self):
        self.now = 0.0
        self.noise = random.Random(SEED)
        self.link = {}
        self.arrived = {}
        self.counted = {}
        self.expected = {}
        self.events = {}
        self.numbers = {}
        self.tasks = []
        self.log = []

    def number(self, name):
        return self.numbers.setdefault(name, len(self.numbers))

    def add(self, task, rank=0):
        rank += self.noise.choice(NOISE)
        self.tasks.append([rank, len(self.log), task, None])
        self.log.append(rank)
        self.step(self.tasks[-1])

    def sent(self, key, axis, d, size):
        hops = min(d % SIZE[axis], -d % SIZE[axis]) if axis != "c" else 0
        if axis == "w":
            dx, dy = d % NX, d // NX
            far = min(dx, NX - dx) + min(dy, NY - dy)
            self.arrived[key] = max(self.arrived.get(key, 0.0), self.now + 2.3 + 0.6 * far)
            self.counted[key] = self.counted.get(key, 0) + size
            return
        if axis == "c":
            paths, load = [axis], size / RATE_CHIP
        elif 2 * hops == SIZE[axis]:
            paths, load = [(axis, 1), (axis, -1)], size * hops / 2 / RATE
        else:
            paths, load = [(axis, 1 if d % SIZE[axis] == hops else -1)], size * hops / RATE
        start = max([self.now] + [self.link.get(path, 0.0) for path in paths])
        for path in paths:
            self.link[path] = start + load
        came = start + load + DELAY[axis, hops]
        self.arrived[key] = max(self.arrived.get(key, 0.0), came)
        self.counted[key] = self.counted.get(key, 0) + size

    def mark(self, name):
        self.events[name] = self.now

    def ready(self, need):
        if need is None:
            return 0.0
        if need[0] == "r":
            if self.counted.get(need[1], 0) < need[2]:
                return NEVER
            return self.arrived[need[1]]
        return max(self.events.get(name, NEVER) for name in need[1])

    def step(self, entry):
        try:
            entry[3] = next(entry[2])
        except StopIteration:
            self.tasks.remove(entry)

    def run(self):
        while self.tasks:
            times = [self.ready(entry[3]) for entry in self.tasks]
            first = min(times)
            if first >= NEVER:
                raise ValueError("stuck")
            self.now = max(self.now, first)
            able = [e for e, t in zip(self.tasks, times) if t <= self.now]
            best = min(able, key=lambda e: (e[0], self.ready(e[3]), e[1]))
            self.step(best)


def rows_a(way, part):
    return pl.ds(0 if way == 1 else 8, 8) if part else pl.ds(0, 16)


def rows_b(way, part):
    if not part:
        return pl.ds(16, 24)
    return pl.ds(16, 16) if way == 1 else pl.ds(32, 8)


def ii(way):
    return 0 if way == 1 else 1


def kernel_body(k_hbm, traces_hbm, ids_ref, counts_ref, sol_out, left_out, *scratch):
    (traces, kf, s3, sp, kt3, pick, p, vall, vh, vl, wst, uall, q, acc, tbuf, tsend, meta, mbuf,
     send_e, recv_e1, send_e2, recv_e2, rza1, rza2, ryb, rzb1, rzb2, rya, rxq, dummy, tiny, nown, nx, nz,
     left, ostage, orecv, ssem, rsem, lsem) = scratch
    plan = Plan()
    r = lax.axis_index("rec")
    s = lax.axis_index("src")
    z, y = r // NY, r % NY
    x, c = s // 2, s % 2
    oc = 1 - c
    me = {"x": x, "y": y, "z": z}

    def at(axis, d):
        return lax.rem(me[axis] + d + 2 * SIZE[axis], SIZE[axis])

    def dev(axis, d):
        zz = at("z", d) if axis == "z" else z
        yy = at("y", d // NX if axis == "w" else d) if axis in "yw" else y
        xx = at("x", d % NX if axis == "w" else d) if axis in "xw" else x
        return (zz * NY + yy, xx * 2 + (oc if axis == "c" else c))

    pending = {}
    groups = {}

    def size_of(ref):
        size = 4
        for n in ref.shape:
            size *= n
        return size

    def waiting(size, i, sems):
        rows = (dummy if size % 4096 == 0 else tiny).at[pl.ds(0, size // 512)]
        return pltpu.make_async_copy(rows, rows, sems.at[i])

    def send(it, name, src, dst, axis, d, group):
        i = plan.number(name)
        g = groups.setdefault(group, len(groups))
        pltpu.make_async_remote_copy(
            src_ref=src, dst_ref=dst, send_sem=ssem.at[g], recv_sem=rsem.at[i],
            device_id=dev(axis, d), device_id_type=MESH).start()
        pending[group] = pending.get(group, 0) + size_of(src)
        plan.sent((it, name), axis, d, size_of(src))

    def wait_recv(it, name, size):
        yield ("r", (it, name), size)
        waiting(size, plan.number(name), rsem).wait()

    def flush(*names):
        for group in names:
            size = pending.pop(group, 0)
            if size:
                waiting(size, groups[group], ssem).wait()

    def need(*names):
        return ("e", names)

    def spend(us):
        plan.now += us

    own_k = pltpu.make_async_copy(k_hbm.at[:, c], kf.at[:, c], lsem.at[0])
    own_k.start()
    own_t = pltpu.make_async_copy(traces_hbm, traces, lsem.at[1])
    own_t.start()
    barrier = pltpu.get_barrier_semaphore()
    friends = [(a, d) for a in ("z", "w") for d in range(1, SIZE[a])] + [("c", 0)]
    for friend in friends:
        pl.semaphore_signal(barrier, inc=1, device_id=dev(*friend), device_id_type=MESH)

    slots = traces_hbm.shape[1]
    lane_row = lax.broadcasted_iota(jnp.int32, (1, slots), 1)
    listed = jnp.where(lane_row < counts_ref[...], ids_ref[...], -1)
    meta[...] = jnp.full((8, 128), -1, jnp.int32)

    @pl.when(c == 0)
    def _():
        meta[0:1, 0:slots] = listed

    @pl.when(c == 1)
    def _():
        meta[0:1, 32:32 + slots] = listed

    blank = jnp.zeros((32, HALVES * LANES), F32)
    tbuf[pl.ds(pl.multiple_of(c * 32, 32), 32), :] = blank
    tsend[...] = blank
    own_t.wait()
    for half in range(HALVES):
        for part in range(2):
            cols = slice(half * LANES + part * WIDE, half * LANES + part * WIDE + WIDE)
            lanes = slice(half * WIDE, half * WIDE + WIDE)
            slab0 = traces[0, :, part, 0, lanes]
            slab1 = traces[0, :, part, 1, lanes]
            tsend[0:slots, cols] = jnp.where(c == 0, slab1, slab0)
            tbuf[pl.ds(pl.multiple_of(c * 32, 32), slots), cols] = jnp.where(c == 0, slab0, slab1)
    pl.semaphore_wait(barrier, len(friends))
    send(0, "meta", meta, mbuf, "c", 0, "in")
    send(0, "traces", tsend, tbuf.at[pl.ds(c * 32, 32)], "c", 0, "in")
    send(0, "k", k_hbm.at[:, oc], kf.at[:, c], "c", 0, "in")

    row = lax.broadcasted_iota(jnp.int32, (64, 128), 0)
    lane = lax.broadcasted_iota(jnp.int32, (64, 128), 1)
    wide = HALVES * LANES

    def observe():
        yield from wait_recv(0, "meta", 4096)
        yield from wait_recv(0, "traces", size_of(tsend))
        ids = jnp.maximum(meta[0:1, :], mbuf[0:1, :])
        area = (row >> 3) * NY + (row & 3)
        offset = ids - ROWS * area
        match = (offset >= 0) & (offset < ROWS) & ((lane >> 5) == ((row >> 2) & 1))
        picked = jnp.dot(jnp.where(match, 1.0, 0.0)[:, :64], tbuf[...],
                         preferred_element_type=F32, precision=EXACT)
        place = jnp.sum(jnp.where(match, (offset + 1).astype(F32), 0.0), axis=1, keepdims=True)
        send_e[:, :, 0:wide] = picked.reshape(NZ, 8, wide)
        send_e[:, :, wide:] = jnp.broadcast_to(place, (64, 128)).reshape(NZ, 8, 128)
        spend(0.8)
        mine = pl.ds(pl.multiple_of(z * 8, 8), 8)
        for d in (4, 3, 5, 2, 6, 1, 7):
            send(0, "e1", send_e.at[at("z", d)], recv_e1.at[mine], "z", d, "in")
        recv_e1[mine, :] = send_e[z]
        yield from wait_recv(0, "e1", 7 * size_of(send_e.at[0]))
        swap = jnp.where(lane == (row & 15) * 4 + (row >> 4), 1.0, 0.0)[:, :64]
        send_e2[...] = jnp.dot(swap, recv_e1[...], preferred_element_type=F32,
                               precision=EXACT).reshape(NY, 16, wide + 128)
        spend(0.8)
        for d in (2, 1, 3):
            send(0, "e2", send_e2.at[at("y", d)], recv_e2.at[y], "y", d, "in")
        recv_e2[y] = send_e2[y]
        yield from wait_recv(0, "e2", 3 * size_of(send_e2.at[0]))
        got = recv_e2[...].reshape(64, wide + 128)
        slot = got[:, wide:]
        wanted = slot - 1.0 + jnp.where((row & 1) == 1, float(ROWS), 0.0)
        onehot = jnp.where((slot > 0.5) & (lane.astype(F32) == wanted), 1.0, 0.0)
        value = jnp.dot(jnp.transpose(onehot)[:BLK, :], got[:, :wide],
                        preferred_element_type=F32, precision=EXACT)
        spend(0.8)
        for h in range(HALVES):
            left[h] = value[:, h * LANES:h * LANES + LANES]
            plan.mark(("left", 0, h))

    def split_half(half):
        for part in range(2):
            cols = pl.ds(pl.multiple_of(half * 640, 128), 640)
            value = kf[part, half]
            high = value.astype(BF16)
            low = (value - high.astype(F32)).astype(BF16)
            base = part * ROWS_REC
            s3[base:base + ROWS_REC, cols] = high
            s3[base + 320:base + 320 + ROWS_REC, cols] = low
            s3[base + 640:base + 640 + ROWS_REC, cols] = high

    dims = (((1,), (1,)), ((), ()))

    def order_kernel():
        def build(i, carry):
            start = pl.multiple_of(i * 256, 256)
            new = lax.broadcasted_iota(jnp.int32, (256, 128), 0) + start
            rec = (new * 1639) >> 16
            rest = new - rec * BLK
            old = jnp.where(rest >= ROWS, 640 - ROWS, 0) + rec * ROWS + rest
            lanes = lax.broadcasted_iota(jnp.int32, (256, 128), 1)
            for j in range(COLS // 128):
                pick[pl.ds(start, 256), j * 128:j * 128 + 128] = jnp.where(
                    lanes + j * 128 == old, 1.0, 0.0).astype(BF16)
            return carry

        lax.fori_loop(0, COLS // 256, build, 0)
        spend(1.5)
        own_k.wait()
        split_half(c)
        spend(0.4)
        yield from wait_recv(0, "k", size_of(kf.at[:, 0]))
        split_half(oc)
        spend(0.4)

        def turned(i, carry):
            start = pl.multiple_of(i * 256, 256)
            kt3[pl.ds(start, 256), :] = lax.dot_general(
                pick[pl.ds(start, 256), :], s3[...], dims, preferred_element_type=F32).astype(BF16)
            return carry

        for low, high in ((0, 2), (2, 4), (4, 5)):
            lax.fori_loop(low, high, turned, 0)
            spend(0.8 * (high - low))
            plan.mark(("kt3", low))
            yield need(("kt3", low))
        plan.mark("kt3")

        def straight(i, carry):
            start = pl.multiple_of(i * 256, 256)
            sp[:, pl.ds(start, 256)] = lax.dot_general(
                s3[0:640, :], pick[pl.ds(start, 256), :], dims, preferred_element_type=F32).astype(BF16)
            return carry

        yield need(("p", 0, HALVES - 1))
        for i in range(COLS // 256):
            lax.fori_loop(i, i + 1, straight, 0)
            spend(0.65)
            plan.mark(("sp", i))
            yield need(("sp", i))
        plan.mark("sp")

    def squares(value):
        squared = value * value
        total = squared[0:8, 0:128]
        for a in range(BLK // 8):
            for b in range(LANES // 128):
                if a or b:
                    total = total + squared[a * 8:a * 8 + 8, b * 128:b * 128 + 128]
        return total

    sums = {}

    def norm(kind, it, axes):
        yield need(*[("sum", kind, it, h) for h in range(HALVES)])
        total = sums[kind, it, 0]
        for h in range(1, HALVES):
            total = total + sums[kind, it, h]
        total = jnp.sum(total, axis=0, keepdims=True)
        flush(("n", kind))
        for axis in axes:
            buf = {"w": nx, "z": nz}[axis]
            size = SIZE[axis]
            mine = z if axis == "z" else y * NX + x
            nown[kind, "wz".index(axis)] = total
            buf[kind, mine] = total
            for d in range(1, size):
                send(it, ("n", kind, axis), nown.at[kind, "wz".index(axis)], buf.at[kind, mine],
                     axis, d, ("n", kind))
            yield from wait_recv(it, ("n", kind, axis), (size - 1) * 512)
            total = buf[kind, 0]
            for i in range(1, size):
                total = total + buf[kind, i]
            spend(0.1)
        sums[kind, it] = jnp.sqrt(jnp.sum(total, axis=(0, 1), keepdims=True) / COUNT)
        spend(0.2)
        plan.mark(("norm", kind, it))

    def gather_x(it, h):
        yield need(("left", it, h))
        flush(("gx", h))
        value = left[h]
        uall[h, x] = value
        for d in (2, 1, 3):
            send(it, ("gx", h), uall.at[h, x], uall.at[h, x], "x", d, ("gx", h))
        sums[0, it, h] = squares(value)
        spend(0.15)
        plan.mark(("sum", 0, it, h))
        yield from wait_recv(it, ("gx", h), 3 * size_of(uall.at[h, 0]))
        plan.mark(("gx", it, h))
        yield need("kt3")
        flush(("gr", h), ("sx", h))
        value = uall[h].reshape(ROWS_REC, LANES)
        real, imag = value[:, :WIDE], value[:, WIDE:]
        for base, both in ((0, (real, imag)), (ROWS_REC, (imag, -real))):
            for i in range(2):
                cols = slice(i * WIDE, i * WIDE + WIDE)
                high = both[i].astype(BF16)
                wst[base:base + ROWS_REC, cols] = high
                wst[base + 320:base + 320 + ROWS_REC, cols] = high
                wst[base + 640:base + 640 + ROWS_REC, cols] = (both[i] - high.astype(F32)).astype(BF16)

        def tile(i, carry):
            start = pl.multiple_of(i * 640, 640)
            out = jnp.dot(kt3[pl.ds(start, 640), :], wst[...], preferred_element_type=F32)
            p[h, pl.ds(i * 4, 4)] = out.reshape(4, NY, BLK, LANES)
            return carry

        lax.fori_loop(0, 2, tile, 0)
        spend(1.2)
        plan.mark(("p", it, h))

    ORDER = (4, 3, 5, 2, 6, 1, 7, 0)
    A, B = pl.ds(0, 16), pl.ds(16, 24)

    def za(it, h):
        yield need(("p", it, h))
        if h in ZA_RELAY:
            yield need(*[("zr", it, h, g) for g in range(2)])
        else:
            for way in WAYS:
                part = rows_a(way, True)
                send(it, ("za", h, way), p.at[h, at("z", 3 * way), :, A], rza1.at[h, ii(way), :, pl.ds(0, 16)],
                     "z", way, ("sr", h))
                send(it, ("za", h, way), p.at[h, at("z", 4 * way), :, part], rza1.at[h, ii(way), :, pl.ds(16, 8)],
                     "z", 2 * way, ("sr", h))
            for way in WAYS:
                send(it, ("za", h), p.at[h, at("z", way), :, A], rza2.at[h, ii(way)], "z", way, ("sr", h))
            for way in WAYS:
                yield from wait_recv(it, ("za", h, way), size_of(rza1.at[h, 0]))
                p[h, at("z", 2 * way), :, A] += rza1[h, ii(way), :, 0:16]
                p[h, at("z", 2 * way), :, rows_a(way, True)] += rza1[h, ii(way), :, 16:24]
                spend(0.12)
                send(it, ("za", h), p.at[h, at("z", 2 * way), :, A], rza2.at[h, 2 + ii(way)], "z", 2 * way, ("sr", h))
            yield from wait_recv(it, ("za", h), size_of(rza2.at[h]))
            p[h, z, :, A] += rza2[h, 0] + rza2[h, 1] + rza2[h, 2] + rza2[h, 3]
        spend(0.15)
        for d in (2, 1, 3):
            send(it, ("ya", h), p.at[h, z, at("y", d), A], rya.at[h, d - 1], "y", d, ("sr", h))
        yield from wait_recv(it, ("ya", h), size_of(rya.at[h]))
        p[h, z, y, A] += rya[h, 0] + rya[h, 1] + rya[h, 2]
        spend(0.06)
        plan.mark(("za", it, h))

    def zr(it, h, g):
        yield need(("p", it, h))
        pair = pl.ds(2 * g, 2)
        for way in WAYS:
            part = rows_a(way, True)
            send(it, ("zr", h, g, way, 1), p.at[h, at("z", 4 * way), pair, part],
                 rza1.at[h, ii(way), pair, pl.ds(16, 8)], "z", way, ("sr", h))
        for step in (1, 2, 3):
            for way in WAYS:
                part = rows_a(way, True)
                yield from wait_recv(it, ("zr", h, g, way, step), (16 if step == 1 else 32) * 4 * LANES)
                d = at("z", (4 - step) * way)
                if step == 1:
                    p[h, d, pair, part] += rza1[h, ii(way), pair, 16:24]
                elif step == 2:
                    p[h, d, pair, A] += rza1[h, ii(way), pair, 0:16]
                else:
                    p[h, d, pair, A] += rza2[h, 2 + ii(way), pair]
                spend(0.06)
                into = (None, rza1.at[h, ii(way), pair, pl.ds(0, 16)], rza2.at[h, 2 + ii(way), pair],
                        rza2.at[h, ii(way), pair])[step]
                name = ("zr", h, g, way, step + 1) if step < 3 else ("zr", h, g)
                send(it, name, p.at[h, d, pair, A], into, "z", way, ("sr", h))
        yield from wait_recv(it, ("zr", h, g), 2 * 32 * 4 * LANES)
        p[h, z, pair, A] += rza2[h, 0, pair] + rza2[h, 1, pair]
        spend(0.08)
        plan.mark(("zr", it, h, g))

    def yb(it, h, d):
        k = ORDER.index(d)
        if k < AHEAD:
            yield need(("p", it, h))
        else:
            yield need(("yb", it, h, ORDER[k - AHEAD]))
        if d in YB_RELAY:
            for way in WAYS:
                part = rows_b(way if d % 2 else -way, True)
                send(it, ("yb", h, d, way), p.at[h, at("z", d), at("y", 2), part],
                     ryb.at[h, d, 2, pl.ds(part.start - 16, part.size)], "y", way, ("sr", h))
            for way in WAYS:
                part = rows_b(way if d % 2 else -way, True)
                yield from wait_recv(it, ("yb", h, d, way), part.size * 4 * LANES)
                p[h, at("z", d), at("y", way), part] += ryb[h, d, 2, part.start - 16:part.start - 16 + part.size]
                spend(0.05)
                send(it, ("yb", h, d), p.at[h, at("z", d), at("y", way), B], ryb.at[h, d, ii(way)], "y", way, ("sr", h))
            yield from wait_recv(it, ("yb", h, d), 2 * 24 * 4 * LANES)
            p[h, at("z", d), y, B] += ryb[h, d, 0] + ryb[h, d, 1]
        else:
            for e in (2, 1, 3):
                send(it, ("yb", h, d), p.at[h, at("z", d), at("y", e), B], ryb.at[h, d, e - 1], "y", e, ("sr", h))
            yield from wait_recv(it, ("yb", h, d), size_of(ryb.at[h, 0]))
            p[h, at("z", d), y, B] += ryb[h, d, 0] + ryb[h, d, 1] + ryb[h, d, 2]
        spend(0.08)
        plan.mark(("yb", it, h, d))

    def zb(it, h, way):
        part = rows_b(way, True)
        yield need(("yb", it, h, 4))
        send(it, ("zb", h, way), p.at[h, at("z", 4 * way), y, part], rzb1.at[h, ii(way), pl.ds(24, part.size)],
             "z", 2 * way, ("sr", h))
        yield need(("yb", it, h, 3 * way % NZ))
        send(it, ("zb", h, way), p.at[h, at("z", 3 * way), y, B], rzb1.at[h, ii(way), pl.ds(0, 24)],
             "z", way, ("sr", h))
        yield need(("yb", it, h, 2 * way % NZ))
        yield from wait_recv(it, ("zb", h, way), (24 + part.size) * 4 * LANES)
        p[h, at("z", 2 * way), y, B] += rzb1[h, ii(way), 0:24]
        p[h, at("z", 2 * way), y, part] += rzb1[h, ii(way), 24:24 + part.size]
        spend(0.06)
        send(it, ("zb", h), p.at[h, at("z", 2 * way), y, B], rzb2.at[h, 2 + ii(way)], "z", 2 * way, ("sr", h))
        plan.mark(("zb", it, h, way))

    def zb_end(it, h):
        for way in WAYS:
            yield need(("yb", it, h, way % NZ))
            send(it, ("zb", h), p.at[h, at("z", way), y, B], rzb2.at[h, ii(way)], "z", way, ("sr", h))
        yield need(("yb", it, h, 0), *[("zb", it, h, way) for way in WAYS])
        yield from wait_recv(it, ("zb", h), size_of(rzb2.at[h]))
        p[h, z, y, B] += rzb2[h, 0] + rzb2[h, 1] + rzb2[h, 2] + rzb2[h, 3]
        spend(0.08)
        plan.mark(("zb", it, h))

    state = {}

    def right(it, h):
        yield need(("norm", 0, it), ("za", it, h), ("zb", it, h))
        beta = sums[0, it]
        value = p[h, z, y] / beta
        if it:
            value = value - beta * state["v", h]
        vall[h, z, y] = value
        state["right", h] = value
        spend(0.1)
        plan.mark(("right", it, h))
        sums[1, it, h] = squares(value)
        spend(0.15)
        plan.mark(("sum", 1, it, h))

    def bz(it, h):
        yield need(("right", it, h))
        own = vall.at[h, z, y, B]
        for d in (2, -2, 1, -1):
            send(it, ("bz", h, -d % NZ), own, own, "z", d, ("gr", h))
        for way in WAYS:
            yield from wait_recv(it, ("bz", h, -2 * way % NZ), 24 * 4 * LANES)
            block = vall.at[h, at("z", -2 * way), y, rows_b(way, True)]
            send(it, ("bz", h, 4), block, block, "z", 2 * way, ("gr", h))
            block = vall.at[h, at("z", -2 * way), y, B]
            send(it, ("bz", h, -3 * way % NZ), block, block, "z", way, ("gr", h))
            plan.mark(("bz", it, h, -2 * way % NZ))

    def by(it, h, d):
        if d == 0:
            yield need(("right", it, h))
        elif d in (2, 6):
            yield need(("bz", it, h, d))
        else:
            yield from wait_recv(it, ("bz", h, d), 24 * 4 * LANES)
        block = vall.at[h, at("z", d), y, B]
        if d in BY_RELAY:
            for way in WAYS:
                send(it, ("by", h, d, way), block, block, "y", way, ("gr", h))
            plan.mark(("by", it, h, d))
            for way in WAYS:
                yield from wait_recv(it, ("by", h, d, way), 24 * 4 * LANES)
                block = vall.at[h, at("z", d), at("y", -way), rows_b(way if d % 2 else -way, True)]
                send(it, ("by", h), block, block, "y", way, ("gr", h))
        else:
            for e in (2, 1, 3):
                send(it, ("by", h), block, block, "y", e, ("gr", h))
        plan.mark(("by", it, h, d))

    def ar(it, h, g):
        yield need(("ay", it, h))
        pair = pl.ds(2 * g, 2)
        own = vall.at[h, z, pair, A]
        for way in WAYS:
            send(it, ("ar", h, g, way, 1), own, own, "z", way, ("gr", h))
        for step in (1, 2, 3):
            for way in WAYS:
                yield from wait_recv(it, ("ar", h, g, way, step), 32 * 4 * LANES)
                rows = A if step < 3 else rows_a(way, True)
                block = vall.at[h, at("z", -way * step), pair, rows]
                send(it, ("ar", h, g, way, step + 1) if step < 3 else ("ar", h, g), block, block, "z", way, ("gr", h))
        yield from wait_recv(it, ("ar", h, g), 32 * 4 * LANES)
        plan.mark(("ar", it, h, g))

    def az(it, h):
        yield need(("right", it, h))
        own = vall.at[h, z, y, A]
        for d in (2, 1, 3):
            send(it, ("ay", h), own, own, "y", d, ("gr", h))
        yield from wait_recv(it, ("ay", h), 3 * 16 * 4 * LANES)
        plan.mark(("ay", it, h))
        if h in AZ_RELAY:
            yield need(*[("ar", it, h, g) for g in range(2)])
            plan.mark(("az", it, h))
            return
        own = vall.at[h, z, :, A]
        for d in (2, -2):
            send(it, ("az", h, d), own, own, "z", d, ("gr", h))
        for d in (1, -1):
            send(it, ("az", h), own, own, "z", d, ("gr", h))
        for way in WAYS:
            yield from wait_recv(it, ("az", h, 2 * way), 64 * 4 * LANES)
            block = vall.at[h, at("z", -2 * way), :, A]
            send(it, ("az", h), block, block, "z", way, ("gr", h))
            block = vall.at[h, at("z", -2 * way), :, rows_a(way, True)]
            send(it, ("az", h), block, block, "z", 2 * way, ("gr", h))
        yield from wait_recv(it, ("az", h), 5 * 64 * 4 * LANES)
        plan.mark(("az", it, h))

    def forward(it, h):
        yield need("sp", ("az", it, h), *[("by", it, h, d) for d in range(NZ)])
        yield from wait_recv(it, ("by", h), (NZ * 3 - 2 * len(BY_RELAY)) * 24 * 4 * LANES)
        flush(("gx", h), ("sr", h))

        def parts(i, carry):
            value = vall[h, i].reshape(NY * BLK, LANES)
            high = value.astype(BF16)
            rows = pl.ds(pl.multiple_of(i * 160, 160), 160)
            vh[rows, :] = high
            vl[rows, :] = (value - high.astype(F32)).astype(BF16)
            return carry

        lax.fori_loop(0, NZ, parts, 0)

        def tile(i, carry):
            rows = pl.ds(pl.multiple_of(i * 320, 320), 320)
            acc[rows, :] = jnp.dot(sp[rows, :], vh[...], preferred_element_type=F32)
            return carry

        lax.fori_loop(0, 2, tile, 0)
        both = acc[0:320, :] + acc[320:640, :] + jnp.dot(sp[0:320, :], vl[...], preferred_element_type=F32)
        real = both[:ROWS_REC, :WIDE] - both[ROWS_REC:, WIDE:]
        imag = both[:ROWS_REC, WIDE:] + both[ROWS_REC:, :WIDE]
        q[h, :, :, :WIDE] = real.reshape(NX, BLK, WIDE)
        q[h, :, :, WIDE:] = imag.reshape(NX, BLK, WIDE)
        spend(1.4)
        for d in (2, 1, 3):
            send(it, ("sx", h), q.at[h, at("x", d)], rxq.at[h, d - 1], "x", d, ("sx", h))
        yield from wait_recv(it, ("sx", h), size_of(rxq.at[h]))
        product = q[h, x] + rxq[h, 0] + rxq[h, 1] + rxq[h, 2]
        yield need(("norm", 1, it))
        alpha, beta = sums[1, it], sums[0, it]
        value = product / alpha - alpha * (left[h] / beta)
        left[h] = value
        spend(0.15)
        plan.mark(("left", it + 1, h))
        vnew = state["right", h] / alpha
        if it == 0:
            state["w", h] = vnew
            state["sol", h] = jnp.zeros((BLK, LANES), F32)
        else:
            rho, cosine, sine, phibar = rotation(it - 1)
            state["sol", h] = state["sol", h] + (cosine * phibar / rho) * state["w", h]
            state["w", h] = vnew - (sine * alpha / rho) * state["w", h]
        state["v", h] = vnew
        spend(0.3)
        plan.mark(("state", it, h))

    known = {}

    def rotation(it):
        if it not in known:
            beta = sums[0, it + 1]
            if it == 0:
                rhobar, phibar = sums[1, 0], sums[0, 0]
            else:
                rho, cosine, sine, phibar = rotation(it - 1)
                rhobar, phibar = -cosine * sums[1, it], sine * phibar
            rho = jnp.sqrt(rhobar * rhobar + beta * beta)
            known[it] = (rho, rhobar / rho, beta / rho, phibar)
        return known[it]

    def output(i, h, out):
        if i == 0:
            yield need(("left", ITERS, h))
            value = left[h]
            sums[0, ITERS, h] = squares(value)
            plan.mark(("sum", 0, ITERS, h))
        else:
            yield need(("norm", 0, ITERS), ("state", ITERS - 1, h))
            rho, cosine, sine, phibar = rotation(ITERS - 1)
            value = state["sol", h] + (cosine * phibar / rho) * state["w", h]
        ostage[i, h, 0, 0:ROWS] = value[:ROWS]
        ostage[i, h, 1, 0:ROWS] = value[ROWS:]
        spend(0.2)
        send(0, ("out", i, h), ostage.at[i, h, oc], orecv.at[i, h], "c", 0, "out")
        yield from wait_recv(0, ("out", i, h), size_of(orecv.at[i, h]))
        mine = ostage[i, h, c, 0:ROWS]
        other = orecv[i, h, 0:ROWS]
        slab = (jnp.where(c == 0, mine, other), jnp.where(c == 0, other, mine))
        for f in range(FREQS):
            for part in range(2):
                out[:, part, f, h * WIDE:h * WIDE + WIDE] = slab[f][:, part * WIDE:part * WIDE + WIDE]
        spend(0.2)

    plan.add(observe(), 0)
    for it in range(ITERS):
        plan.add(norm(0, it, "wz"), 0)
        plan.add(norm(1, it, "zw"), 0)
        for h in range(HALVES):
            plan.add(gather_x(it, h), 1 + h)
            plan.add(za(it, h), 1 + h)
            plan.add(zb_end(it, h), 1 + h)
            plan.add(bz(it, h), 1 + h)
            plan.add(az(it, h), 1 + h)
            for g in range(2):
                if h in ZA_RELAY:
                    plan.add(zr(it, h, g), 1 + h)
                if h in AZ_RELAY:
                    plan.add(ar(it, h, g), 1 + h)
            for way in WAYS:
                plan.add(zb(it, h, way), 1 + h)
            for d in ORDER:
                plan.add(yb(it, h, d), 1 + h)
            for d in (0, 1, 7, 2, 6, 3, 5, 4):
                plan.add(by(it, h, d), 1 + h)
            plan.add(right(it, h), 1 + h)
            plan.add(forward(it, h), 1 + h)
    plan.add(norm(0, ITERS, "wz"), 0)
    for h in range(HALVES):
        plan.add(output(0, h, left_out), 3)
        plan.add(output(1, h, sol_out), 2)
    plan.add(order_kernel(), 5)
    plan.run()
    flush(*list(pending))
    TOTAL.append((plan.now, dict(plan.events), (len(plan.numbers), len(groups))))


TOTAL = []


def hand_over(sol_in, left_in, sol_out, left_out):
    sol_out[...] = sol_in[...]
    left_out[...] = left_in[...]


def on_device(kernel, traces, acq_lists, counts):
    vmem = pltpu.VMEM
    two = HALVES
    scratch = [
        vmem(traces.shape, F32),
        vmem((2, 2, ROWS_REC, 640), F32),
        vmem((960, COLS), BF16),
        vmem((640, COLS), BF16),
        vmem((COLS, 960), BF16),
        vmem((COLS, COLS), BF16),
        vmem((two, NZ, NY, BLK, LANES), F32),
        vmem((two, NZ, NY, BLK, LANES), F32),
        vmem((COLS, LANES), BF16),
        vmem((COLS, LANES), BF16),
        vmem((960, LANES), BF16),
        vmem((two, NX, BLK, LANES), F32),
        vmem((two, NX, BLK, LANES), F32),
        vmem((640, LANES), F32),
        vmem((64, two * LANES), F32),
        vmem((32, two * LANES), F32),
        vmem((8, 128), jnp.int32),
        vmem((8, 128), jnp.int32),
        vmem((NZ, 8, two * LANES + 128), F32),
        vmem((64, two * LANES + 128), F32),
        vmem((NY, 16, two * LANES + 128), F32),
        vmem((NY, 16, two * LANES + 128), F32),
        vmem((two, 2, NY, 24, LANES), F32),
        vmem((two, 4, NY, 16, LANES), F32),
        vmem((two, NZ, 3, 24, LANES), F32),
        vmem((two, 2, 40, LANES), F32),
        vmem((two, 4, 24, LANES), F32),
        vmem((two, 3, 16, LANES), F32),
        vmem((two, 3, BLK, LANES), F32),
        vmem((8192, 128), F32),
        vmem((64, 1, 128), F32),
        vmem((2, 2, 1, 128), F32),
        vmem((2, NX * NY, 1, 128), F32),
        vmem((2, NZ, 1, 128), F32),
        vmem((two, BLK, LANES), F32),
        vmem((2, two, 2, 24, LANES), F32),
        vmem((2, two, 24, LANES), F32),
        pltpu.SemaphoreType.DMA((GROUPS,)),
        pltpu.SemaphoreType.DMA((COPIES,)),
        pltpu.SemaphoreType.DMA((2,)),
    ]
    whole = pl.BlockSpec(memory_space=pltpu.VMEM)
    made = pl.pallas_call(
        kernel_body,
        out_shape=(jax.ShapeDtypeStruct((ROWS, 2, FREQS, SOURCES), F32),) * 2,
        in_specs=[pl.BlockSpec(memory_space=pl.ANY)] * 2 + [whole, whole],
        out_specs=(whole, whole),
        scratch_shapes=scratch,
        compiler_params=pltpu.CompilerParams(
            collective_id=0, has_side_effects=True, vmem_limit_bytes=60 * 1024 * 1024),
    )(kernel, traces, acq_lists, counts)
    return pl.pallas_call(
        hand_over,
        out_shape=(jax.ShapeDtypeStruct((ROWS, 2, FREQS, SOURCES), F32),) * 2,
        in_specs=[whole, whole],
        out_specs=(whole, whole),
    )(*made)


def solution(mesh):
    placed = (
        P(None, None, "rec", "src"),
        P("src", "rec", None, None, None),
        P("src", "rec"),
        P("src", "rec"),
    )
    return jax.shard_map(
        on_device,
        mesh=mesh,
        in_specs=placed,
        out_specs=(P(("src", "rec"), None, None, None), P(("rec", "src"), None, None, None)),
        check_vma=False,
    )
```

```python
import random
import jax
import jax.numpy as jnp
from jax import lax
from jax.experimental import pallas as pl
from jax.experimental.pallas import tpu as pltpu
from jax.sharding import PartitionSpec as P

NR = 5120
FREQS = 2
SOURCES = 256
ITERS = 2
NZ, NY, NX = 8, 4, 4
SIZE = {"x": NX, "y": NY, "z": NZ, "w": NX * NY}
ROWS = 20
HALVES = 2
WIDE = SOURCES // HALVES
LANES = 2 * WIDE
BLK = 40
ROWS_REC = 160
COLS = 1280
COPIES = 71
GROUPS = 16
AHEAD = 4
SEED = 0
NOISE = (0,)
ZA_RELAY = ()
AZ_RELAY = ()
YB_RELAY = ()
BY_RELAY = ()
MESH = pl.DeviceIdType.MESH
F32 = jnp.float32
BF16 = jnp.bfloat16
COUNT = 2.0 * NR * SOURCES
EXACT = lax.Precision.HIGHEST
NEVER = 1e9

RATE = 51e3
RATE_CHIP = 600e3
DELAY = {("c", 0): 0.9, ("z", 1): 1.9, ("z", 2): 2.5, ("z", 3): 3.1, ("z", 4): 3.7}
DELAY.update({(a, d): 2.2 + 0.2 * d for a in "xy" for d in (1, 2)})
WAYS = (1, -1)


class Plan:
    def __init__(self):
        self.now = 0.0
        self.noise = random.Random(SEED)
        self.link = {}
        self.arrived = {}
        self.counted = {}
        self.expected = {}
        self.events = {}
        self.numbers = {}
        self.tasks = []
        self.log = []

    def number(self, name):
        return self.numbers.setdefault(name, len(self.numbers))

    def add(self, task, rank=0):
        rank += self.noise.choice(NOISE)
        self.tasks.append([rank, len(self.log), task, None])
        self.log.append(rank)
        self.step(self.tasks[-1])

    def sent(self, key, axis, d, size):
        hops = min(d % SIZE[axis], -d % SIZE[axis]) if axis != "c" else 0
        if axis == "w":
            dx, dy = d % NX, d // NX
            far = min(dx, NX - dx) + min(dy, NY - dy)
            self.arrived[key] = max(self.arrived.get(key, 0.0), self.now + 2.3 + 0.6 * far)
            self.counted[key] = self.counted.get(key, 0) + size
            return
        if axis == "c":
            paths, load = [axis], size / RATE_CHIP
        elif 2 * hops == SIZE[axis]:
            paths, load = [(axis, 1), (axis, -1)], size * hops / 2 / RATE
        else:
            paths, load = [(axis, 1 if d % SIZE[axis] == hops else -1)], size * hops / RATE
        start = max([self.now] + [self.link.get(path, 0.0) for path in paths])
        for path in paths:
            self.link[path] = start + load
        came = start + load + DELAY[axis, hops]
        self.arrived[key] = max(self.arrived.get(key, 0.0), came)
        self.counted[key] = self.counted.get(key, 0) + size

    def mark(self, name):
        self.events[name] = self.now

    def ready(self, need):
        if need is None:
            return 0.0
        if need[0] == "r":
            if self.counted.get(need[1], 0) < need[2]:
                return NEVER
            return self.arrived[need[1]]
        return max(self.events.get(name, NEVER) for name in need[1])

    def step(self, entry):
        try:
            entry[3] = next(entry[2])
        except StopIteration:
            self.tasks.remove(entry)

    def run(self):
        while self.tasks:
            times = [self.ready(entry[3]) for entry in self.tasks]
            first = min(times)
            if first >= NEVER:
                raise ValueError("stuck")
            self.now = max(self.now, first)
            able = [e for e, t in zip(self.tasks, times) if t <= self.now]
            best = min(able, key=lambda e: (e[0], self.ready(e[3]), e[1]))
            self.step(best)


def rows_a(way, part):
    return pl.ds(0 if way == 1 else 8, 8) if part else pl.ds(0, 16)


def rows_b(way, part):
    if not part:
        return pl.ds(16, 24)
    return pl.ds(16, 16) if way == 1 else pl.ds(32, 8)


def ii(way):
    return 0 if way == 1 else 1


def kernel_body(k_hbm, traces_hbm, ids_ref, counts_ref, sol_out, left_out, *scratch):
    (traces, kf, s3, sp, kt3, pick, p, vall, vh, vl, wst, uall, q, acc, tbuf, tsend, meta, mbuf,
     send_e, recv_e1, send_e2, recv_e2, rza1, rza2, ryb, rzb1, rzb2, rya, rxq, dummy, tiny, nown, nx, nz,
     left, ostage, orecv, ssem, rsem, lsem) = scratch
    plan = Plan()
    r = lax.axis_index("rec")
    s = lax.axis_index("src")
    z, y = r // NY, r % NY
    x, c = s // 2, s % 2
    oc = 1 - c
    me = {"x": x, "y": y, "z": z}

    def at(axis, d):
        return lax.rem(me[axis] + d + 2 * SIZE[axis], SIZE[axis])

    def dev(axis, d):
        zz = at("z", d) if axis == "z" else z
        yy = at("y", d // NX if axis == "w" else d) if axis in "yw" else y
        xx = at("x", d % NX if axis == "w" else d) if axis in "xw" else x
        return (zz * NY + yy, xx * 2 + (oc if axis == "c" else c))

    pending = {}
    groups = {}

    def size_of(ref):
        size = 4
        for n in ref.shape:
            size *= n
        return size

    def waiting(size, i, sems):
        rows = (dummy if size % 4096 == 0 else tiny).at[pl.ds(0, size // 512)]
        return pltpu.make_async_copy(rows, rows, sems.at[i])

    def send(it, name, src, dst, axis, d, group):
        i = plan.number(name)
        g = groups.setdefault(group, len(groups))
        pltpu.make_async_remote_copy(
            src_ref=src, dst_ref=dst, send_sem=ssem.at[g], recv_sem=rsem.at[i],
            device_id=dev(axis, d), device_id_type=MESH).start()
        pending[group] = pending.get(group, 0) + size_of(src)
        plan.sent((it, name), axis, d, size_of(src))

    def wait_recv(it, name, size):
        yield ("r", (it, name), size)
        waiting(size, plan.number(name), rsem).wait()

    def flush(*names):
        for group in names:
            size = pending.pop(group, 0)
            if size:
                waiting(size, groups[group], ssem).wait()

    def need(*names):
        return ("e", names)

    def spend(us):
        plan.now += us

    own_k = pltpu.make_async_copy(k_hbm.at[:, c], kf.at[:, c], lsem.at[0])
    own_k.start()
    own_t = pltpu.make_async_copy(traces_hbm, traces, lsem.at[1])
    own_t.start()
    barrier = pltpu.get_barrier_semaphore()
    friends = [(a, d) for a in ("z", "w") for d in range(1, SIZE[a])] + [("c", 0)]
    for friend in friends:
        pl.semaphore_signal(barrier, inc=1, device_id=dev(*friend), device_id_type=MESH)

    slots = traces_hbm.shape[1]
    lane_row = lax.broadcasted_iota(jnp.int32, (1, slots), 1)
    listed = jnp.where(lane_row < counts_ref[...], ids_ref[...], -1)
    meta[...] = jnp.full((8, 128), -1, jnp.int32)

    @pl.when(c == 0)
    def _():
        meta[0:1, 0:slots] = listed

    @pl.when(c == 1)
    def _():
        meta[0:1, 32:32 + slots] = listed

    blank = jnp.zeros((32, HALVES * LANES), F32)
    tbuf[pl.ds(pl.multiple_of(c * 32, 32), 32), :] = blank
    tsend[...] = blank
    own_t.wait()
    for half in range(HALVES):
        for part in range(2):
            cols = slice(half * LANES + part * WIDE, half * LANES + part * WIDE + WIDE)
            lanes = slice(half * WIDE, half * WIDE + WIDE)
            slab0 = traces[0, :, part, 0, lanes]
            slab1 = traces[0, :, part, 1, lanes]
            tsend[0:slots, cols] = jnp.where(c == 0, slab1, slab0)
            tbuf[pl.ds(pl.multiple_of(c * 32, 32), slots), cols] = jnp.where(c == 0, slab0, slab1)
    pl.semaphore_wait(barrier, len(friends))
    send(0, "meta", meta, mbuf, "c", 0, "in")
    send(0, "traces", tsend, tbuf.at[pl.ds(c * 32, 32)], "c", 0, "in")
    send(0, "k", k_hbm.at[:, oc], kf.at[:, c], "c", 0, "in")

    row = lax.broadcasted_iota(jnp.int32, (64, 128), 0)
    lane = lax.broadcasted_iota(jnp.int32, (64, 128), 1)
    wide = HALVES * LANES

    def observe():
        yield from wait_recv(0, "meta", 4096)
        yield from wait_recv(0, "traces", size_of(tsend))
        ids = jnp.maximum(meta[0:1, :], mbuf[0:1, :])
        area = (row >> 3) * NY + (row & 3)
        offset = ids - ROWS * area
        match = (offset >= 0) & (offset < ROWS) & ((lane >> 5) == ((row >> 2) & 1))
        picked = jnp.dot(jnp.where(match, 1.0, 0.0)[:, :64], tbuf[...],
                         preferred_element_type=F32, precision=EXACT)
        place = jnp.sum(jnp.where(match, (offset + 1).astype(F32), 0.0), axis=1, keepdims=True)
        send_e[:, :, 0:wide] = picked.reshape(NZ, 8, wide)
        send_e[:, :, wide:] = jnp.broadcast_to(place, (64, 128)).reshape(NZ, 8, 128)
        spend(0.8)
        mine = pl.ds(pl.multiple_of(z * 8, 8), 8)
        for d in (4, 3, 5, 2, 6, 1, 7):
            send(0, "e1", send_e.at[at("z", d)], recv_e1.at[mine], "z", d, "in")
        recv_e1[mine, :] = send_e[z]
        yield from wait_recv(0, "e1", 7 * size_of(send_e.at[0]))
        swap = jnp.where(lane == (row & 15) * 4 + (row >> 4), 1.0, 0.0)[:, :64]
        send_e2[...] = jnp.dot(swap, recv_e1[...], preferred_element_type=F32,
                               precision=EXACT).reshape(NY, 16, wide + 128)
        spend(0.8)
        for d in (2, 1, 3):
            send(0, "e2", send_e2.at[at("y", d)], recv_e2.at[y], "y", d, "in")
        recv_e2[y] = send_e2[y]
        yield from wait_recv(0, "e2", 3 * size_of(send_e2.at[0]))
        got = recv_e2[...].reshape(64, wide + 128)
        slot = got[:, wide:]
        wanted = slot - 1.0 + jnp.where((row & 1) == 1, float(ROWS), 0.0)
        onehot = jnp.where((slot > 0.5) & (lane.astype(F32) == wanted), 1.0, 0.0)
        value = jnp.dot(jnp.transpose(onehot)[:BLK, :], got[:, :wide],
                        preferred_element_type=F32, precision=EXACT)
        spend(0.8)
        for h in range(HALVES):
            left[h] = value[:, h * LANES:h * LANES + LANES]
            plan.mark(("left", 0, h))

    def split_half(half):
        for part in range(2):
            cols = pl.ds(pl.multiple_of(half * 640, 128), 640)
            value = kf[part, half]
            high = value.astype(BF16)
            low = (value - high.astype(F32)).astype(BF16)
            base = part * ROWS_REC
            s3[base:base + ROWS_REC, cols] = high
            s3[base + 320:base + 320 + ROWS_REC, cols] = low
            s3[base + 640:base + 640 + ROWS_REC, cols] = high

    dims = (((1,), (1,)), ((), ()))

    def order_kernel():
        def build(i, carry):
            start = pl.multiple_of(i * 256, 256)
            new = lax.broadcasted_iota(jnp.int32, (256, 128), 0) + start
            rec = (new * 1639) >> 16
            rest = new - rec * BLK
            old = jnp.where(rest >= ROWS, 640 - ROWS, 0) + rec * ROWS + rest
            lanes = lax.broadcasted_iota(jnp.int32, (256, 128), 1)
            for j in range(COLS // 128):
                pick[pl.ds(start, 256), j * 128:j * 128 + 128] = jnp.where(
                    lanes + j * 128 == old, 1.0, 0.0).astype(BF16)
            return carry

        lax.fori_loop(0, COLS // 256, build, 0)
        spend(1.5)
        own_k.wait()
        split_half(c)
        spend(0.4)
        yield from wait_recv(0, "k", size_of(kf.at[:, 0]))
        split_half(oc)
        spend(0.4)

        def turned(i, carry):
            start = pl.multiple_of(i * 256, 256)
            kt3[pl.ds(start, 256), :] = lax.dot_general(
                pick[pl.ds(start, 256), :], s3[...], dims, preferred_element_type=F32).astype(BF16)
            return carry

        for low, high in ((0, 2), (2, 4), (4, 5)):
            lax.fori_loop(low, high, turned, 0)
            spend(0.8 * (high - low))
            plan.mark(("kt3", low))
            yield need(("kt3", low))
        plan.mark("kt3")

        def straight(i, carry):
            start = pl.multiple_of(i * 256, 256)
            sp[:, pl.ds(start, 256)] = lax.dot_general(
                s3[0:640, :], pick[pl.ds(start, 256), :], dims, preferred_element_type=F32).astype(BF16)
            return carry

        yield need(("p", 0, HALVES - 1))
        for i in range(COLS // 256):
            lax.fori_loop(i, i + 1, straight, 0)
            spend(0.65)
            plan.mark(("sp", i))
            yield need(("sp", i))
        plan.mark("sp")

    def squares(value):
        squared = value * value
        total = squared[0:8, 0:128]
        for a in range(BLK // 8):
            for b in range(LANES // 128):
                if a or b:
                    total = total + squared[a * 8:a * 8 + 8, b * 128:b * 128 + 128]
        return total

    sums = {}

    def norm(kind, it, axes):
        yield need(*[("sum", kind, it, h) for h in range(HALVES)])
        total = sums[kind, it, 0]
        for h in range(1, HALVES):
            total = total + sums[kind, it, h]
        total = jnp.sum(total, axis=0, keepdims=True)
        flush(("n", kind))
        for axis in axes:
            buf = {"w": nx, "z": nz}[axis]
            size = SIZE[axis]
            mine = z if axis == "z" else y * NX + x
            nown[kind, "wz".index(axis)] = total
            buf[kind, mine] = total
            for d in range(1, size):
                send(it, ("n", kind, axis), nown.at[kind, "wz".index(axis)], buf.at[kind, mine],
                     axis, d, ("n", kind))
            yield from wait_recv(it, ("n", kind, axis), (size - 1) * 512)
            total = buf[kind, 0]
            for i in range(1, size):
                total = total + buf[kind, i]
            spend(0.1)
        sums[kind, it] = jnp.sqrt(jnp.sum(total, axis=(0, 1), keepdims=True) / COUNT)
        spend(0.2)
        plan.mark(("norm", kind, it))

    def gather_x(it, h):
        yield need(("left", it, h))
        flush(("gx", h))
        value = left[h]
        uall[h, x] = value
        for d in (2, 1, 3):
            send(it, ("gx", h), uall.at[h, x], uall.at[h, x], "x", d, ("gx", h))
        sums[0, it, h] = squares(value)
        spend(0.15)
        plan.mark(("sum", 0, it, h))
        yield from wait_recv(it, ("gx", h), 3 * size_of(uall.at[h, 0]))
        plan.mark(("gx", it, h))
        yield need("kt3")
        flush(("gr", h), ("sx", h))
        value = uall[h].reshape(ROWS_REC, LANES)
        real, imag = value[:, :WIDE], value[:, WIDE:]
        for base, both in ((0, (real, imag)), (ROWS_REC, (imag, -real))):
            for i in range(2):
                cols = slice(i * WIDE, i * WIDE + WIDE)
                high = both[i].astype(BF16)
                wst[base:base + ROWS_REC, cols] = high
                wst[base + 320:base + 320 + ROWS_REC, cols] = high
                wst[base + 640:base + 640 + ROWS_REC, cols] = (both[i] - high.astype(F32)).astype(BF16)

        def tile(i, carry):
            start = pl.multiple_of(i * 640, 640)
            out = jnp.dot(kt3[pl.ds(start, 640), :], wst[...], preferred_element_type=F32)
            p[h, pl.ds(i * 4, 4)] = out.reshape(4, NY, BLK, LANES)
            return carry

        lax.fori_loop(0, 2, tile, 0)
        spend(1.2)
        plan.mark(("p", it, h))

    ORDER = (4, 3, 5, 2, 6, 1, 7, 0)
    A, B = pl.ds(0, 16), pl.ds(16, 24)

    def za(it, h):
        yield need(("p", it, h))
        if h in ZA_RELAY:
            yield need(*[("zr", it, h, g) for g in range(2)])
        else:
            for way in WAYS:
                part = rows_a(way, True)
                send(it, ("za", h, way), p.at[h, at("z", 3 * way), :, A], rza1.at[h, ii(way), :, pl.ds(0, 16)],
                     "z", way, ("sr", h))
                send(it, ("za", h, way), p.at[h, at("z", 4 * way), :, part], rza1.at[h, ii(way), :, pl.ds(16, 8)],
                     "z", 2 * way, ("sr", h))
            for way in WAYS:
                send(it, ("za", h), p.at[h, at("z", way), :, A], rza2.at[h, ii(way)], "z", way, ("sr", h))
            for way in WAYS:
                yield from wait_recv(it, ("za", h, way), size_of(rza1.at[h, 0]))
                p[h, at("z", 2 * way), :, A] += rza1[h, ii(way), :, 0:16]
                p[h, at("z", 2 * way), :, rows_a(way, True)] += rza1[h, ii(way), :, 16:24]
                spend(0.12)
                send(it, ("za", h), p.at[h, at("z", 2 * way), :, A], rza2.at[h, 2 + ii(way)], "z", 2 * way, ("sr", h))
            yield from wait_recv(it, ("za", h), size_of(rza2.at[h]))
            p[h, z, :, A] += rza2[h, 0] + rza2[h, 1] + rza2[h, 2] + rza2[h, 3]
        spend(0.15)
        for d in (2, 1, 3):
            send(it, ("ya", h), p.at[h, z, at("y", d), A], rya.at[h, d - 1], "y", d, ("sr", h))
        yield from wait_recv(it, ("ya", h), size_of(rya.at[h]))
        p[h, z, y, A] += rya[h, 0] + rya[h, 1] + rya[h, 2]
        spend(0.06)
        plan.mark(("za", it, h))

    def zr(it, h, g):
        yield need(("p", it, h))
        pair = pl.ds(2 * g, 2)
        for way in WAYS:
            part = rows_a(way, True)
            send(it, ("zr", h, g, way, 1), p.at[h, at("z", 4 * way), pair, part],
                 rza1.at[h, ii(way), pair, pl.ds(16, 8)], "z", way, ("sr", h))
        for step in (1, 2, 3):
            for way in WAYS:
                part = rows_a(way, True)
                yield from wait_recv(it, ("zr", h, g, way, step), (16 if step == 1 else 32) * 4 * LANES)
                d = at("z", (4 - step) * way)
                if step == 1:
                    p[h, d, pair, part] += rza1[h, ii(way), pair, 16:24]
                elif step == 2:
                    p[h, d, pair, A] += rza1[h, ii(way), pair, 0:16]
                else:
                    p[h, d, pair, A] += rza2[h, 2 + ii(way), pair]
                spend(0.06)
                into = (None, rza1.at[h, ii(way), pair, pl.ds(0, 16)], rza2.at[h, 2 + ii(way), pair],
                        rza2.at[h, ii(way), pair])[step]
                name = ("zr", h, g, way, step + 1) if step < 3 else ("zr", h, g)
                send(it, name, p.at[h, d, pair, A], into, "z", way, ("sr", h))
        yield from wait_recv(it, ("zr", h, g), 2 * 32 * 4 * LANES)
        p[h, z, pair, A] += rza2[h, 0, pair] + rza2[h, 1, pair]
        spend(0.08)
        plan.mark(("zr", it, h, g))

    def yb(it, h, d):
        k = ORDER.index(d)
        if k < AHEAD:
            yield need(("p", it, h))
        else:
            yield need(("yb", it, h, ORDER[k - AHEAD]))
        if d in YB_RELAY:
            for way in WAYS:
                part = rows_b(way if d % 2 else -way, True)
                send(it, ("yb", h, d, way), p.at[h, at("z", d), at("y", 2), part],
                     ryb.at[h, d, 2, pl.ds(part.start - 16, part.size)], "y", way, ("sr", h))
            for way in WAYS:
                part = rows_b(way if d % 2 else -way, True)
                yield from wait_recv(it, ("yb", h, d, way), part.size * 4 * LANES)
                p[h, at("z", d), at("y", way), part] += ryb[h, d, 2, part.start - 16:part.start - 16 + part.size]
                spend(0.05)
                send(it, ("yb", h, d), p.at[h, at("z", d), at("y", way), B], ryb.at[h, d, ii(way)], "y", way, ("sr", h))
            yield from wait_recv(it, ("yb", h, d), 2 * 24 * 4 * LANES)
            p[h, at("z", d), y, B] += ryb[h, d, 0] + ryb[h, d, 1]
        else:
            for e in (2, 1, 3):
                send(it, ("yb", h, d), p.at[h, at("z", d), at("y", e), B], ryb.at[h, d, e - 1], "y", e, ("sr", h))
            yield from wait_recv(it, ("yb", h, d), size_of(ryb.at[h, 0]))
            p[h, at("z", d), y, B] += ryb[h, d, 0] + ryb[h, d, 1] + ryb[h, d, 2]
        spend(0.08)
        plan.mark(("yb", it, h, d))

    def zb(it, h, way):
        part = rows_b(way, True)
        yield need(("yb", it, h, 4))
        send(it, ("zb", h, way), p.at[h, at("z", 4 * way), y, part], rzb1.at[h, ii(way), pl.ds(24, part.size)],
             "z", 2 * way, ("sr", h))
        yield need(("yb", it, h, 3 * way % NZ))
        send(it, ("zb", h, way), p.at[h, at("z", 3 * way), y, B], rzb1.at[h, ii(way), pl.ds(0, 24)],
             "z", way, ("sr", h))
        yield need(("yb", it, h, 2 * way % NZ))
        yield from wait_recv(it, ("zb", h, way), (24 + part.size) * 4 * LANES)
        p[h, at("z", 2 * way), y, B] += rzb1[h, ii(way), 0:24]
        p[h, at("z", 2 * way), y, part] += rzb1[h, ii(way), 24:24 + part.size]
        spend(0.06)
        send(it, ("zb", h), p.at[h, at("z", 2 * way), y, B], rzb2.at[h, 2 + ii(way)], "z", 2 * way, ("sr", h))
        plan.mark(("zb", it, h, way))

    def zb_end(it, h):
        for way in WAYS:
            yield need(("yb", it, h, way % NZ))
            send(it, ("zb", h), p.at[h, at("z", way), y, B], rzb2.at[h, ii(way)], "z", way, ("sr", h))
        yield need(("yb", it, h, 0), *[("zb", it, h, way) for way in WAYS])
        yield from wait_recv(it, ("zb", h), size_of(rzb2.at[h]))
        p[h, z, y, B] += rzb2[h, 0] + rzb2[h, 1] + rzb2[h, 2] + rzb2[h, 3]
        spend(0.08)
        plan.mark(("zb", it, h))

    state = {}

    def right(it, h):
        yield need(("norm", 0, it), ("za", it, h), ("zb", it, h))
        beta = sums[0, it]
        value = p[h, z, y] / beta
        if it:
            value = value - beta * state["v", h]
        vall[h, z, y] = value
        state["right", h] = value
        spend(0.1)
        plan.mark(("right", it, h))
        sums[1, it, h] = squares(value)
        spend(0.15)
        plan.mark(("sum", 1, it, h))

    def bz(it, h):
        yield need(("right", it, h))
        own = vall.at[h, z, y, B]
        for d in (2, -2, 1, -1):
            send(it, ("bz", h, -d % NZ), own, own, "z", d, ("gr", h))
        for way in WAYS:
            yield from wait_recv(it, ("bz", h, -2 * way % NZ), 24 * 4 * LANES)
            block = vall.at[h, at("z", -2 * way), y, rows_b(way, True)]
            send(it, ("bz", h, 4), block, block, "z", 2 * way, ("gr", h))
            block = vall.at[h, at("z", -2 * way), y, B]
            send(it, ("bz", h, -3 * way % NZ), block, block, "z", way, ("gr", h))
            plan.mark(("bz", it, h, -2 * way % NZ))

    def by(it, h, d):
        if d == 0:
            yield need(("right", it, h))
        elif d in (2, 6):
            yield need(("bz", it, h, d))
        else:
            yield from wait_recv(it, ("bz", h, d), 24 * 4 * LANES)
        block = vall.at[h, at("z", d), y, B]
        if d in BY_RELAY:
            for way in WAYS:
                send(it, ("by", h, d, way), block, block, "y", way, ("gr", h))
            plan.mark(("by", it, h, d))
            for way in WAYS:
                yield from wait_recv(it, ("by", h, d, way), 24 * 4 * LANES)
                block = vall.at[h, at("z", d), at("y", -way), rows_b(way if d % 2 else -way, True)]
                send(it, ("by", h), block, block, "y", way, ("gr", h))
        else:
            for e in (2, 1, 3):
                send(it, ("by", h), block, block, "y", e, ("gr", h))
        plan.mark(("by", it, h, d))

    def ar(it, h, g):
        yield need(("ay", it, h))
        pair = pl.ds(2 * g, 2)
        own = vall.at[h, z, pair, A]
        for way in WAYS:
            send(it, ("ar", h, g, way, 1), own, own, "z", way, ("gr", h))
        for step in (1, 2, 3):
            for way in WAYS:
                yield from wait_recv(it, ("ar", h, g, way, step), 32 * 4 * LANES)
                rows = A if step < 3 else rows_a(way, True)
                block = vall.at[h, at("z", -way * step), pair, rows]
                send(it, ("ar", h, g, way, step + 1) if step < 3 else ("ar", h, g), block, block, "z", way, ("gr", h))
        yield from wait_recv(it, ("ar", h, g), 32 * 4 * LANES)
        plan.mark(("ar", it, h, g))

    def az(it, h):
        yield need(("right", it, h))
        own = vall.at[h, z, y, A]
        for d in (2, 1, 3):
            send(it, ("ay", h), own, own, "y", d, ("gr", h))
        yield from wait_recv(it, ("ay", h), 3 * 16 * 4 * LANES)
        plan.mark(("ay", it, h))
        if h in AZ_RELAY:
            yield need(*[("ar", it, h, g) for g in range(2)])
            plan.mark(("az", it, h))
            return
        own = vall.at[h, z, :, A]
        for d in (2, -2):
            send(it, ("az", h, d), own, own, "z", d, ("gr", h))
        for d in (1, -1):
            send(it, ("az", h), own, own, "z", d, ("gr", h))
        for way in WAYS:
            yield from wait_recv(it, ("az", h, 2 * way), 64 * 4 * LANES)
            block = vall.at[h, at("z", -2 * way), :, A]
            send(it, ("az", h), block, block, "z", way, ("gr", h))
            block = vall.at[h, at("z", -2 * way), :, rows_a(way, True)]
            send(it, ("az", h), block, block, "z", 2 * way, ("gr", h))
        yield from wait_recv(it, ("az", h), 5 * 64 * 4 * LANES)
        plan.mark(("az", it, h))

    def forward(it, h):
        yield need("sp", ("az", it, h), *[("by", it, h, d) for d in range(NZ)])
        yield from wait_recv(it, ("by", h), (NZ * 3 - 2 * len(BY_RELAY)) * 24 * 4 * LANES)
        flush(("gx", h), ("sr", h))

        def parts(i, carry):
            value = vall[h, i].reshape(NY * BLK, LANES)
            high = value.astype(BF16)
            rows = pl.ds(pl.multiple_of(i * 160, 160), 160)
            vh[rows, :] = high
            vl[rows, :] = (value - high.astype(F32)).astype(BF16)
            return carry

        lax.fori_loop(0, NZ, parts, 0)

        acc[...] = jnp.dot(sp[...], vh[...], preferred_element_type=F32)
        both = acc[0:320, :] + acc[320:640, :] + jnp.dot(sp[0:320, :], vl[...], preferred_element_type=F32)
        real = both[:ROWS_REC, :WIDE] - both[ROWS_REC:, WIDE:]
        imag = both[:ROWS_REC, WIDE:] + both[ROWS_REC:, :WIDE]
        q[h, :, :, :WIDE] = real.reshape(NX, BLK, WIDE)
        q[h, :, :, WIDE:] = imag.reshape(NX, BLK, WIDE)
        spend(1.4)
        for d in (2, 1, 3):
            send(it, ("sx", h), q.at[h, at("x", d)], rxq.at[h, d - 1], "x", d, ("sx", h))
        yield from wait_recv(it, ("sx", h), size_of(rxq.at[h]))
        product = q[h, x] + rxq[h, 0] + rxq[h, 1] + rxq[h, 2]
        yield need(("norm", 1, it))
        alpha, beta = sums[1, it], sums[0, it]
        value = product / alpha - alpha * (left[h] / beta)
        left[h] = value
        spend(0.15)
        plan.mark(("left", it + 1, h))
        vnew = state["right", h] / alpha
        if it == 0:
            state["w", h] = vnew
            state["sol", h] = jnp.zeros((BLK, LANES), F32)
        else:
            rho, cosine, sine, phibar = rotation(it - 1)
            state["sol", h] = state["sol", h] + (cosine * phibar / rho) * state["w", h]
            state["w", h] = vnew - (sine * alpha / rho) * state["w", h]
        state["v", h] = vnew
        spend(0.3)
        plan.mark(("state", it, h))

    known = {}

    def rotation(it):
        if it not in known:
            beta = sums[0, it + 1]
            if it == 0:
                rhobar, phibar = sums[1, 0], sums[0, 0]
            else:
                rho, cosine, sine, phibar = rotation(it - 1)
                rhobar, phibar = -cosine * sums[1, it], sine * phibar
            rho = jnp.sqrt(rhobar * rhobar + beta * beta)
            known[it] = (rho, rhobar / rho, beta / rho, phibar)
        return known[it]

    def output(i, h, out):
        if i == 0:
            yield need(("left", ITERS, h))
            value = left[h]
            sums[0, ITERS, h] = squares(value)
            plan.mark(("sum", 0, ITERS, h))
        else:
            yield need(("norm", 0, ITERS), ("state", ITERS - 1, h))
            rho, cosine, sine, phibar = rotation(ITERS - 1)
            value = state["sol", h] + (cosine * phibar / rho) * state["w", h]
        ostage[i, h, 0, 0:ROWS] = value[:ROWS]
        ostage[i, h, 1, 0:ROWS] = value[ROWS:]
        spend(0.2)
        send(0, ("out", i, h), ostage.at[i, h, oc], orecv.at[i, h], "c", 0, "out")
        yield from wait_recv(0, ("out", i, h), size_of(orecv.at[i, h]))
        mine = ostage[i, h, c, 0:ROWS]
        other = orecv[i, h, 0:ROWS]
        slab = (jnp.where(c == 0, mine, other), jnp.where(c == 0, other, mine))
        for f in range(FREQS):
            for part in range(2):
                out[:, part, f, h * WIDE:h * WIDE + WIDE] = slab[f][:, part * WIDE:part * WIDE + WIDE]
        spend(0.2)

    plan.add(observe(), 0)
    for it in range(ITERS):
        plan.add(norm(0, it, "wz"), 0)
        plan.add(norm(1, it, "zw"), 0)
        for h in range(HALVES):
            plan.add(gather_x(it, h), 1 + h)
            plan.add(za(it, h), 1 + h)
            plan.add(zb_end(it, h), 1 + h)
            plan.add(bz(it, h), 1 + h)
            plan.add(az(it, h), 1 + h)
            for g in range(2):
                if h in ZA_RELAY:
                    plan.add(zr(it, h, g), 1 + h)
                if h in AZ_RELAY:
                    plan.add(ar(it, h, g), 1 + h)
            for way in WAYS:
                plan.add(zb(it, h, way), 1 + h)
            for d in ORDER:
                plan.add(yb(it, h, d), 1 + h)
            for d in (0, 1, 7, 2, 6, 3, 5, 4):
                plan.add(by(it, h, d), 1 + h)
            plan.add(right(it, h), 1 + h)
            plan.add(forward(it, h), 1 + h)
    plan.add(norm(0, ITERS, "wz"), 0)
    for h in range(HALVES):
        plan.add(output(0, h, left_out), 3)
        plan.add(output(1, h, sol_out), 2)
    plan.add(order_kernel(), 5)
    plan.run()
    flush(*list(pending))
    TOTAL.append((plan.now, dict(plan.events), (len(plan.numbers), len(groups))))


TOTAL = []


def hand_over(sol_in, left_in, sol_out, left_out):
    sol_out[...] = sol_in[...]
    left_out[...] = left_in[...]


def on_device(kernel, traces, acq_lists, counts):
    vmem = pltpu.VMEM
    two = HALVES
    scratch = [
        vmem(traces.shape, F32),
        vmem((2, 2, ROWS_REC, 640), F32),
        vmem((960, COLS), BF16),
        vmem((640, COLS), BF16),
        vmem((COLS, 960), BF16),
        vmem((COLS, COLS), BF16),
        vmem((two, NZ, NY, BLK, LANES), F32),
        vmem((two, NZ, NY, BLK, LANES), F32),
        vmem((COLS, LANES), BF16),
        vmem((COLS, LANES), BF16),
        vmem((960, LANES), BF16),
        vmem((two, NX, BLK, LANES), F32),
        vmem((two, NX, BLK, LANES), F32),
        vmem((640, LANES), F32),
        vmem((64, two * LANES), F32),
        vmem((32, two * LANES), F32),
        vmem((8, 128), jnp.int32),
        vmem((8, 128), jnp.int32),
        vmem((NZ, 8, two * LANES + 128), F32),
        vmem((64, two * LANES + 128), F32),
        vmem((NY, 16, two * LANES + 128), F32),
        vmem((NY, 16, two * LANES + 128), F32),
        vmem((two, 2, NY, 24, LANES), F32),
        vmem((two, 4, NY, 16, LANES), F32),
        vmem((two, NZ, 3, 24, LANES), F32),
        vmem((two, 2, 40, LANES), F32),
        vmem((two, 4, 24, LANES), F32),
        vmem((two, 3, 16, LANES), F32),
        vmem((two, 3, BLK, LANES), F32),
        vmem((8192, 128), F32),
        vmem((64, 1, 128), F32),
        vmem((2, 2, 1, 128), F32),
        vmem((2, NX * NY, 1, 128), F32),
        vmem((2, NZ, 1, 128), F32),
        vmem((two, BLK, LANES), F32),
        vmem((2, two, 2, 24, LANES), F32),
        vmem((2, two, 24, LANES), F32),
        pltpu.SemaphoreType.DMA((GROUPS,)),
        pltpu.SemaphoreType.DMA((COPIES,)),
        pltpu.SemaphoreType.DMA((2,)),
    ]
    whole = pl.BlockSpec(memory_space=pltpu.VMEM)
    made = pl.pallas_call(
        kernel_body,
        out_shape=(jax.ShapeDtypeStruct((ROWS, 2, FREQS, SOURCES), F32),) * 2,
        in_specs=[pl.BlockSpec(memory_space=pl.ANY)] * 2 + [whole, whole],
        out_specs=(whole, whole),
        scratch_shapes=scratch,
        compiler_params=pltpu.CompilerParams(
            collective_id=0, has_side_effects=True, vmem_limit_bytes=60 * 1024 * 1024),
    )(kernel, traces, acq_lists, counts)
    return pl.pallas_call(
        hand_over,
        out_shape=(jax.ShapeDtypeStruct((ROWS, 2, FREQS, SOURCES), F32),) * 2,
        in_specs=[whole, whole],
        out_specs=(whole, whole),
    )(*made)


def solution(mesh):
    placed = (
        P(None, None, "rec", "src"),
        P("src", "rec", None, None, None),
        P("src", "rec"),
        P("src", "rec"),
    )
    return jax.shard_map(
        on_device,
        mesh=mesh,
        in_specs=placed,
        out_specs=(P(("src", "rec"), None, None, None), P(("rec", "src"), None, None, None)),
        check_vma=False,
    )
```
